128 devices in a mesh: outer: 8 (over y, core), inner: 4 (over z), head: 4 (over x).
Axes of the slice: x: 4, y: 4, z: 4, core: 2. Of those that a mesh axis runs over, the one named last changes fastest.
Arguments:
- queries: bfloat16 [32768, 4096], P(('outer', 'inner'), 'head'), may hold values from -6 to 6
- keys: bfloat16 [32768, 4096], P(('outer', 'inner'), 'head'), may hold values from -0.046875 to 0.046875
- values: bfloat16 [32768, 4096], P(('outer', 'inner'), 'head'), may hold values from -36 to 36
- out_grad: bfloat16 [32768, 4096], P(('outer', 'inner'), 'head'), may hold values from -6 to 6
- log_key_decay: float32 [32768, 4096], P(('outer', 'inner'), 'head'), may hold values from -0.62 to 0
- value_rate: float32 [4096], P('head'), may hold values from 3.0517579e-06 to 0.05
- norm_gain: float32 [4096], P('head'), may hold values from 0.1 to 1.9
Outputs:
- query_grad: bfloat16 [32768, 4096], P(('outer', 'inner'), 'head')
- key_grad: bfloat16 [32768, 4096], P(('outer', 'inner'), 'head')
- value_grad: bfloat16 [32768, 4096], P(('outer', 'inner'), 'head')
- gain_grad: float32 [4096], P('head')
The draws below stay inside these ranges and needn't reach their ends.
All inputs are finite; a program needn't handle non-finite values.
Results may differ from the reference program's by a relative error of at most 0.001.
Values sent between devices are 32-bit elements; how exact they have to be, the bound alone decides.
No kernel may reach another device: no remote copies, remote signals or barrier semaphores. Data moves between devices by JAX's collectives and lax.ppermute only.
A program may use at most 192 MiB of HBM per device.

```python
import math
import jax
import jax.numpy as jnp
from jax import lax

HEADS = 32
DK = 128
DV = 128
BL = 128
T_DEV = 1024
TOKENS = 32768


def draw_log_key_decay(key, part):
    columns = HEADS * DK
    every_key_row = jax.random.split(key, 7)
    fast_rate = jnp.exp(jax.random.uniform(every_key_row[0], (columns,), jnp.float32, math.log(1.0 / 50.0), math.log(1.0 / 30.0)))
    slow_rate = jnp.exp(jax.random.uniform(every_key_row[1], (columns,), jnp.float32, math.log(0.1 / TOKENS), math.log(1.0 / TOKENS)))
    fast_share = 0.5
    chooser = jax.random.uniform(every_key_row[2], (columns,), jnp.float32)
    decay_rate = jnp.where(chooser < fast_share, fast_rate, slow_rate)
    segments = TOKENS // T_DEV
    segment_factor = jnp.exp(jax.random.uniform(every_key_row[3], (segments, 1, columns), jnp.float32, math.log(0.5), math.log(2.0)))
    jitter = jax.random.uniform(every_key_row[4], (segments, T_DEV, columns), jnp.float32, 0.5, 1.5)
    baseline_decay = -(decay_rate[None, None, :] * jitter * segment_factor).reshape(TOKENS, columns)
    permuted_order = jax.random.permutation(every_key_row[5], TOKENS)
    spike_depth = jax.random.uniform(every_key_row[6], (2,), jnp.float32, 0.22, 0.51)
    token_positions = jnp.arange(TOKENS)
    spike_loss = jnp.where(token_positions == permuted_order[0], -spike_depth[0], 0.0) + jnp.where(token_positions == permuted_order[1], -spike_depth[1], 0.0)
    return baseline_decay + spike_loss[:, None]


def draw_values(key, part):
    columns = HEADS * DV
    every_key_row = jax.random.split(key, 4)
    current_head_index = (jnp.arange(columns) // DV).astype(jnp.float32)
    head_scale = 3.0 ** (current_head_index / (HEADS - 1))
    channel_scale = jnp.exp(jax.random.uniform(every_key_row[0], (columns,), jnp.float32, math.log(0.3), math.log(3.0)))
    per_token_scale = jnp.exp(jax.random.uniform(every_key_row[1], (TOKENS, 1), jnp.float32, math.log(0.5), math.log(2.0)))
    noise = jnp.clip(jax.random.normal(every_key_row[3], (TOKENS, columns), jnp.float32), -4.0, 4.0)
    return (0.5 * noise * channel_scale[None] * per_token_scale * head_scale[None]).astype(jnp.bfloat16)


def levels(rng, extent, cuts, low, top_value):
    def one(dim, blocks):
        heights = jax.random.uniform(jax.random.fold_in(jax.random.fold_in(rng, 6), dim), (blocks,), jnp.float32, low / len(cuts), top_value / len(cuts))
        return jnp.repeat(jnp.exp(heights), extent[dim] // blocks).reshape((-1,) + (1,) * (len(extent) - dim - 1))

    loudness = one(*cuts[0])
    for cut in cuts[1:]:
        loudness = loudness * one(*cut)
    return loudness


def gaussian(key, dims, scale, bound, cuts=(), kind=jnp.bfloat16):
    array = scale * jax.random.normal(key, dims, jnp.float32)
    if cuts:
        array = array * levels(key, dims, cuts, -0.22, 0.18)
    return jnp.clip(array, -bound, bound).astype(kind)


def setup_inputs(seed: int = 0) -> dict:
    key_list = jax.random.split(jax.random.key(seed), 8)
    queries = gaussian(key_list[0], (TOKENS, HEADS * DK), 1.0, 6.0, ((0, 32), (1, 4)))
    keys = gaussian(key_list[1], (TOKENS, HEADS * DK), (1.0 / DK), 0.046875, ((0, 32), (1, 4)))
    values = draw_values(jax.random.fold_in(key_list[7], 71), 0)
    out_grad = gaussian(key_list[3], (TOKENS, HEADS * DV), 1.0, 6.0, ((0, 32), (1, 4)))
    log_key_decay = draw_log_key_decay(jax.random.fold_in(key_list[7], 71), 0)
    value_rate = jnp.clip(jnp.exp(math.log(0.05) - 9.704061 * jax.random.uniform(key_list[5], (HEADS * DV,), jnp.float32) ** levels(key_list[5], (HEADS * DV,), ((0, 4),), -0.2, 0.2)), 3.051757857974735e-06, 0.05)
    norm_gain = jnp.clip(1.0 + 0.18 * jax.random.normal(key_list[6], (HEADS * DV,), jnp.float32), 0.1, 1.9)
    return {"queries": queries, "keys": keys, "values": values, "out_grad": out_grad, "log_key_decay": log_key_decay, "value_rate": value_rate, "norm_gain": norm_gain}


highest = lax.Precision.HIGHEST

def prepare(query_block, key_block, value_block, decay_block, value_log):
    key_cumul = jnp.cumsum(decay_block.astype(jnp.float32), axis=0)
    steps_in = (jnp.arange(BL, dtype=jnp.float32) + 1.0)[:, None, None]
    value_cumul = steps_in * value_log[None]
    query_tilde = query_block.astype(jnp.float32) * jnp.exp(key_cumul)
    key_tilde = key_block.astype(jnp.float32) * jnp.exp(-key_cumul)
    value_tilde = value_block.astype(jnp.float32) * jnp.exp(-value_cumul)
    block_decay = jnp.exp(key_cumul[-1])[:, :, None] * jnp.exp(BL * value_log)[:, None, :]
    return (key_cumul, value_cumul, query_tilde, key_tilde, value_tilde, block_decay)

def reference(queries, keys, values, out_grad, log_key_decay, value_rate, norm_gain):
    block_total = TOKENS // BL
    value_log = -value_rate.reshape(HEADS, DV)
    rows_index = jnp.arange(BL)
    causal_mask = (rows_index[:, None] >= rows_index[None, :]).astype(jnp.float32)
    query_blocks = queries.reshape(block_total, BL, HEADS, DK)
    key_blocks = keys.reshape(block_total, BL, HEADS, DK)
    value_blocks = values.reshape(block_total, BL, HEADS, DV)
    decay_blocks = log_key_decay.reshape(block_total, BL, HEADS, DK)
    zero_state = jnp.zeros((HEADS, DK, DV), jnp.float32)

    def forward_block(state, inputs):
        key_cumul, value_cumul, query_tilde, key_tilde, value_tilde, block_decay = prepare(*inputs, value_log)
        scores = jnp.einsum('thi,shi->hts', query_tilde, key_tilde, precision=highest) * causal_mask
        core = jnp.exp(value_cumul) * (jnp.einsum('thi,hij->thj', query_tilde, state, precision=highest) + jnp.einsum('hts,shj->thj', scores, value_tilde, precision=highest))
        kv_sum = jnp.einsum('shi,shj->hij', key_tilde, value_tilde, precision=highest)
        return (block_decay * state + block_decay * kv_sum, core)
    _, core = lax.scan(forward_block, zero_state, (query_blocks, key_blocks, value_blocks, decay_blocks))
    core = core.reshape(TOKENS, HEADS * DV)
    columns = HEADS * DV
    grad_out = out_grad.astype(jnp.float32)
    weighted = grad_out * norm_gain[None]
    rms = lax.rsqrt(lax.optimization_barrier(jnp.sum(core * core, axis=1)) / columns + 1e-06)
    cross = lax.optimization_barrier(jnp.sum(weighted * core, axis=1))
    core_grad = rms[:, None] * weighted - core * (rms * rms * rms * cross / columns)[:, None]
    gain_grad = lax.optimization_barrier(jnp.sum(grad_out * core * rms[:, None], axis=0)) / math.sqrt(TOKENS)
    grad_blocks = core_grad.reshape(block_total, BL, HEADS, DV)

    def query_block_step(state, inputs):
        query_block, key_block, value_block, decay_block, grad_block = inputs
        key_cumul, value_cumul, query_tilde, key_tilde, value_tilde, block_decay = prepare(query_block, key_block, value_block, decay_block, value_log)
        grad_tilde = grad_block * jnp.exp(value_cumul)
        mixed = jnp.einsum('thj,shj->hts', grad_tilde, value_tilde, precision=highest) * causal_mask
        query_part = jnp.exp(key_cumul) * (jnp.einsum('thj,hij->thi', grad_tilde, state, precision=highest) + jnp.einsum('hts,shi->thi', mixed, key_tilde, precision=highest))
        kv_sum = jnp.einsum('shi,shj->hij', key_tilde, value_tilde, precision=highest)
        return (block_decay * state + block_decay * kv_sum, query_part.astype(jnp.bfloat16))
    _, query_grad = lax.scan(query_block_step, zero_state, (query_blocks, key_blocks, value_blocks, decay_blocks, grad_blocks))

    def adjoint_block(carry, inputs):
        query_block, key_block, value_block, decay_block, grad_block = inputs
        key_cumul, value_cumul, query_tilde, key_tilde, value_tilde, block_decay = prepare(query_block, key_block, value_block, decay_block, value_log)
        grad_tilde = grad_block * jnp.exp(value_cumul)
        mixed = jnp.einsum('thj,shj->hts', grad_tilde, value_tilde, precision=highest) * causal_mask
        scores = jnp.einsum('thi,shi->hts', query_tilde, key_tilde, precision=highest) * causal_mask
        passed = block_decay * carry
        key_part = jnp.exp(-key_cumul) * (jnp.einsum('hts,thi->shi', mixed, query_tilde, precision=highest) + jnp.einsum('shj,hij->shi', value_tilde, passed, precision=highest))
        value_part = jnp.exp(-value_cumul) * (jnp.einsum('hts,thj->shj', scores, grad_tilde, precision=highest) + jnp.einsum('shi,hij->shj', key_tilde, passed, precision=highest))
        new_carry = jnp.einsum('thi,thj->hij', query_tilde, grad_tilde, precision=highest) + passed
        return (new_carry, (key_part.astype(jnp.bfloat16), value_part.astype(jnp.bfloat16)))
    _, (key_grad, value_grad) = lax.scan(adjoint_block, zero_state, (query_blocks, key_blocks, value_blocks, decay_blocks, grad_blocks), reverse=True)
    return (query_grad.reshape(TOKENS, HEADS * DK), key_grad.reshape(TOKENS, HEADS * DK), value_grad.reshape(TOKENS, HEADS * DV), gain_grad)
```

```python
import functools
import math

import jax
import jax.numpy as jnp
from jax import lax
from jax.experimental import pallas as pl
from jax.experimental.pallas import tpu as pltpu
from jax.sharding import PartitionSpec as P

HEADS = 32
D = 128
BL = 128
HALF = BL // 2
EXTRA = 8
VMEM_MIB = 56
TOGETHER = 2
f32 = jnp.float32
bf16 = jnp.bfloat16

NN = (((1,), (0,)), ((), ()))
NT = (((1,), (1,)), ((), ()))
TN = (((0,), (0,)), ((), ()))


def dot(a, b, dims):
    return lax.dot_general(a, b, dims, preferred_element_type=f32)


def pack(x):
    high = x.astype(bf16)
    return jnp.concatenate([high, (x - high.astype(f32)).astype(bf16)], axis=1)


def halves(x):
    return x[:, :D] + x[:, D:]


def nn(a, b):
    return halves(dot(a, jnp.concatenate([b, b], axis=0), NN))


def nt(a, b):
    high, low = b[:, :D], b[:, D:]
    rows_high = jnp.concatenate([high, high], axis=1)
    rows_low = jnp.concatenate([low, low], axis=1)
    return halves(dot(a, jnp.concatenate([rows_high, rows_low], axis=0), NT))


def tn(a, b):
    stacked = jnp.concatenate([a[:, :D], a[:, D:]], axis=0)
    return halves(dot(stacked, jnp.concatenate([b, b], axis=0), TN))


def tn_long(a, b):
    x = dot(a, b, TN)
    return halves(x[:D] + x[D:])


def iota(axis):
    return lax.broadcasted_iota(jnp.int32, (BL, BL), axis)


def causal():
    return iota(0) >= iota(1)


def centred_sum_matrix():
    t, s = iota(0), iota(1)
    later = ((s <= t) & (s >= HALF)).astype(f32)
    earlier = ((s > t) & (s < HALF)).astype(f32)
    return (later - earlier).astype(bf16)


def rows(b):
    return slice(b * BL, (b + 1) * BL)


def value_tables(value_log):
    steps = (iota(0) - (HALF - 1)).astype(f32) * value_log
    return jnp.exp(steps), jnp.exp(-steps)


def cols(h, width=D):
    return slice(h * width, (h + 1) * width)


def last_row(b):
    return slice((b + 1) * BL - 1, (b + 1) * BL)


def before_and_after(c_ref, mid_ref, h, blocks):
    ends = [c_ref[last_row(b), cols(h)] for b in range(blocks)]
    mids = [mid_ref[h, b : b + 1] for b in range(blocks)]
    before, total = [], jnp.zeros((1, D), f32)
    for b in range(blocks):
        before.append(total + mids[b])
        total = before[b] + ends[b]
    after, rest = [None] * blocks, jnp.zeros((1, D), f32)
    for b in reversed(range(blocks)):
        after[b] = rest + ends[b]
        rest = after[b] + mids[b]
    steps = [jnp.exp(ends[b] + mids[b + 1]) for b in range(blocks - 1)]
    return before, after, steps


def columns_of(row_list):
    stacked = jnp.concatenate(row_list, axis=0)
    padded = jnp.concatenate([stacked, jnp.zeros((D - stacked.shape[0], D), f32)], axis=0)
    return jnp.transpose(padded)


def centred_sums(blocks, ld_ref, c_ref, h):
    matrix = centred_sum_matrix()
    matrix = jnp.concatenate([matrix, matrix], axis=1)
    mids = []
    for b in range(0, blocks, 2):
        x, y = pack(ld_ref[rows(b), cols(h)]), pack(ld_ref[rows(b + 1), cols(h)])
        right = jnp.concatenate(
            [
                jnp.concatenate([x[:, :D], y[:, :D]], axis=1),
                jnp.concatenate([x[:, D:], y[:, D:]], axis=1),
            ],
            axis=0,
        )
        c = dot(matrix, right, NN)
        for at in range(2):
            c_at = c[:, cols(at)]
            c_ref[rows(b + at), cols(h)] = c_at
            first = (b + at) * BL
            mids.append(ld_ref[first : first + 1, cols(h)] - c_at[0:1])
    return mids


def state_kernel(blocks, k_ref, v_ref, ld_ref, rate_ref, pay_ref, c_s, kk, vv):
    span = blocks * BL
    all_mids = [centred_sums(blocks, ld_ref, c_s, h) for h in range(TOGETHER)]
    for h in range(TOGETHER):
        value_log = -rate_ref[h]
        _, shrink = value_tables(value_log)
        rest = jnp.zeros((1, D), f32)
        for b in reversed(range(blocks)):
            c = c_s[rows(b), cols(h)]
            after = rest + c[BL - 1 : BL]
            rest = after + all_mids[h][b]
            kk[h, rows(b)] = pack(k_ref[rows(b), cols(h)].astype(f32) * jnp.exp(after - c))
            reach = jnp.exp(value_log * float(span - BL * b - HALF))
            vv[h, rows(b)] = pack(v_ref[rows(b), cols(h)].astype(f32) * (shrink * reach))
        total = tn_long(kk[h], vv[h])
        value_total = value_log * float(span)
        for part in range(4):
            pay_ref[4 * h + part, 0:32] = total[32 * part : 32 * part + 32]
            pay_ref[4 * h + part, 32:40] = jnp.concatenate(
                [pltpu.roll(rest, (D - 32 * part) % D, 1), value_total, jnp.zeros((6, D), f32)],
                axis=0,
            )


def local_kernel(
    blocks, q_ref, k_ref, v_ref, ld_ref, rate_ref,
    core_ref, qd_ref, starts_ref, c_ref, mid_ref, qs, ks, vs, scores, kv,
):
    mask = causal()
    tables = []
    for h in range(TOGETHER):
        mids = centred_sums(blocks, ld_ref, c_ref, h)
        mid_ref[h] = jnp.concatenate(mids, axis=0)
    for h in range(TOGETHER):
        grow, shrink = value_tables(-rate_ref[h])
        before, _, steps = before_and_after(c_ref, mid_ref, h, blocks)
        tables.append((grow, steps))
        for b in range(blocks):
            c = c_ref[rows(b), cols(h)]
            q = q_ref[rows(b), cols(h)].astype(f32) * jnp.exp(c)
            qs[h, rows(b)] = pack(q)
            qd_ref[rows(b), cols(h, 2 * D)] = pack(q * jnp.exp(before[b]))
            ks[h, rows(b)] = pack(k_ref[rows(b), cols(h)].astype(f32) * jnp.exp(-c))
            vs[h, rows(b)] = pack(v_ref[rows(b), cols(h)].astype(f32) * shrink)
    for h in range(TOGETHER):
        for b in range(blocks):
            part = nt(qs[h, rows(b)], ks[h, rows(b)])
            scores[h, rows(b)] = pack(jnp.where(mask, part, 0.0))
    for h in range(TOGETHER):
        for b in range(blocks - 1):
            kv[h, b] = tn(ks[h, rows(b)], vs[h, rows(b)])
    for h in range(TOGETHER):
        key_steps = columns_of(tables[h][1])
        value_step = jnp.exp(-rate_ref[h] * float(BL))
        state = jnp.zeros((D, D), f32)
        for b in range(blocks):
            starts_ref[h, b] = state
            if b < blocks - 1:
                state = (state + kv[h, b]) * (key_steps[:, b : b + 1] * value_step)
    for h in range(TOGETHER):
        for b in range(blocks):
            value, state = vs[h, rows(b)], pack(starts_ref[h, b])
            left = jnp.concatenate([scores[h, rows(b)], qs[h, rows(b)]], axis=1)
            right = jnp.concatenate([value, value, state, state], axis=0)
            core_ref[rows(b), cols(h)] = tables[h][0] * halves(dot(left, right, NN))


def core_kernel(
    blocks, turns, qd_ref, local_ref, grad_ref, state_ref, rate_ref, gain_ref,
    core_ref, sums_ref, squares, crosses,
):
    turn = pl.program_id(0)

    @pl.when(turn == 0)
    def _():
        squares[...] = jnp.zeros_like(squares)
        crosses[...] = jnp.zeros_like(crosses)

    grows, rights = [], []
    for h in range(TOGETHER):
        grows.append(value_tables(-rate_ref[h])[0])
        state = pack(state_ref[h])
        rights.append(jnp.concatenate([state, state], axis=0))
    for b in range(blocks):
        square, cross = squares[rows(b)], crosses[rows(b)]
        for h in range(TOGETHER):
            reach = jnp.exp(-rate_ref[h] * float(BL * b + HALF))
            incoming = halves(dot(qd_ref[rows(b), cols(h, 2 * D)], rights[h], NN))
            core = local_ref[rows(b), cols(h)] + (grows[h] * reach) * incoming
            core_ref[rows(b), cols(h)] = core
            square = square + core * core
            cross = cross + core * (grad_ref[rows(b), cols(h)].astype(f32) * gain_ref[h])
        squares[rows(b)] = square
        crosses[rows(b)] = cross

    @pl.when(turn == turns - 1)
    def _():
        ones = jnp.ones((8, 2 * D), bf16)
        for at, ref in enumerate((squares, crosses)):
            found = [dot(ones, pack(ref[rows(b)]), NT)[0:1] for b in range(blocks)]
            all_found = jnp.concatenate(found, axis=0)
            for copy in range(sums_ref.shape[0]):
                sums_ref[copy, at * blocks : (at + 1) * blocks] = all_found


def grad_kernel(
    blocks, qd_ref, core_ref, grad_ref, sums_ref, rate_ref, gain_ref, pay_ref, factor_ref, gg
):
    turn = pl.program_id(0)
    columns = HEADS * D

    @pl.when(turn == 0)
    def _():
        both = sums_ref[0]
        for copy in range(1, sums_ref.shape[0]):
            both = both + sums_ref[copy]
        rms = lax.rsqrt(both[0:blocks] / columns + 1e-06)
        coef = rms * rms * rms * both[blocks : 2 * blocks] / columns
        for b in range(blocks):
            factor_ref[rows(b), :D] = jnp.transpose(jnp.broadcast_to(rms[b : b + 1], (BL, D)))
            factor_ref[rows(b), D:] = jnp.transpose(jnp.broadcast_to(coef[b : b + 1], (BL, D)))

    for h in range(TOGETHER):
        grow, _ = value_tables(-rate_ref[h])
        gain_sum = jnp.zeros((BL, D), f32)
        for b in range(blocks):
            core = core_ref[rows(b), cols(h)]
            out = grad_ref[rows(b), cols(h)].astype(f32) * factor_ref[rows(b), :D]
            gain_sum = gain_sum + out * core
            g = out * gain_ref[h] - core * factor_ref[rows(b), D:]
            reach = jnp.exp(-rate_ref[h] * float(BL * b + HALF))
            gg[h, rows(b)] = pack(g * (grow * reach))
        total = tn_long(qd_ref[:, cols(h, 2 * D)], gg[h])
        gain_row = jnp.sum(gain_sum, axis=0, keepdims=True)
        for part in range(4):
            pay_ref[4 * h + part, 0:32] = total[32 * part : 32 * part + 32]
            pay_ref[4 * h + part, 32:40] = jnp.concatenate(
                [gain_row, jnp.zeros((7, D), f32)], axis=0
            )


def block_grad_kernel(
    blocks, made, q_ref, k_ref, v_ref, c_ref, mid_ref, core_ref, grad_ref, factor_ref,
    starts_ref, state_ref, rate_ref, gain_ref, *rest,
):
    dq_ref, dk_ref, dv_ref, qs, ks, vs, gs, start, mixed, scores, qg, passed = rest[made:]
    mask = causal()
    tables = []
    for h in range(TOGETHER):
        grow, shrink = value_tables(-rate_ref[h])
        before, _, steps = before_and_after(c_ref, mid_ref, h, blocks)
        key_columns = columns_of(steps + [jnp.exp(x) for x in before])
        tables.append((shrink, key_columns))
        for b in range(blocks):
            c = c_ref[rows(b), cols(h)]
            qs[h, rows(b)] = pack(q_ref[rows(b), cols(h)].astype(f32) * jnp.exp(c))
            ks[h, rows(b)] = pack(k_ref[rows(b), cols(h)].astype(f32) * jnp.exp(-c))
            vs[h, rows(b)] = pack(v_ref[rows(b), cols(h)].astype(f32) * shrink)
            out = grad_ref[rows(b), cols(h)].astype(f32) * factor_ref[rows(b), :D]
            g = out * gain_ref[h] - core_ref[rows(b), cols(h)] * factor_ref[rows(b), D:]
            gs[h, rows(b)] = pack(g * grow)
            at = blocks - 1 + b
            reach = jnp.exp(-rate_ref[h] * float(BL * b + HALF))
            begun = starts_ref[h, b] + state_ref[h] * (key_columns[:, at : at + 1] * reach)
            start[h, rows(b)] = pack(begun)
    for h in range(TOGETHER):
        for b in range(blocks):
            part = nt(gs[h, rows(b)], vs[h, rows(b)])
            mixed[h, rows(b)] = pack(jnp.where(mask, part, 0.0))
            part = nt(qs[h, rows(b)], ks[h, rows(b)])
            scores[h, rows(b)] = pack(jnp.where(mask, part, 0.0))
    for h in range(TOGETHER):
        for b in range(1, blocks):
            qg[h, b] = tn(qs[h, rows(b)], gs[h, rows(b)])
    for h in range(TOGETHER):
        value_step = jnp.exp(-rate_ref[h] * float(BL))
        now = jnp.zeros((D, D), f32)
        for b in reversed(range(blocks)):
            passed[h, rows(b)] = pack(now)
            if b:
                now = (now + qg[h, b]) * (tables[h][1][:, b - 1 : b] * value_step)
    for h in range(TOGETHER):
        for b in range(blocks):
            dq = nn(mixed[h, rows(b)], ks[h, rows(b)]) + nt(gs[h, rows(b)], start[h, rows(b)])
            dq_ref[rows(b), cols(h)] = (jnp.exp(c_ref[rows(b), cols(h)]) * dq).astype(bf16)
    for h in range(TOGETHER):
        for b in range(blocks):
            dk = tn(mixed[h, rows(b)], qs[h, rows(b)]) + nt(vs[h, rows(b)], passed[h, rows(b)])
            dk_ref[rows(b), cols(h)] = jnp.exp(-c_ref[rows(b), cols(h)]) * dk
    for h in range(TOGETHER):
        for b in range(blocks):
            dv = tn(scores[h, rows(b)], gs[h, rows(b)]) + nn(ks[h, rows(b)], passed[h, rows(b)])
            dv_ref[rows(b), cols(h)] = tables[h][0] * dv


def final_kernel(
    blocks, k_ref, v_ref, c_ref, mid_ref, dk_ref, dv_ref, back_ref, rate_ref,
    dk_out, dv_out, gain_out,
):
    span = blocks * BL
    for h in range(TOGETHER):
        value_log = -rate_ref[h]
        _, shrink = value_tables(value_log)
        _, after, _ = before_and_after(c_ref, mid_ref, h, blocks)
        back = pack(back_ref[4 * h : 4 * h + 4, 0:32].reshape(D, D))
        for b in range(blocks):
            at = rows(b), cols(h)
            fade = jnp.exp(after[b] - c_ref[at])
            value_fade = shrink * jnp.exp(value_log * float(span - BL * b - HALF))
            ks = pack(k_ref[at].astype(f32) * fade)
            vs = pack(v_ref[at].astype(f32) * value_fade)
            dk_out[at] = (dk_ref[at] + fade * nt(vs, back)).astype(bf16)
            dv_out[at] = (dv_ref[at] + value_fade * nn(ks, back)).astype(bf16)
        gain_out[h] = back_ref[4 * h, 32:33]


def forward_scan_kernel(count, pay_ref, out_ref, weight_ref):
    decays = jnp.concatenate([pay_ref[s, 32:33] for s in range(count)], axis=0)
    padded = jnp.concatenate([decays, jnp.zeros((D - count, D), f32)], axis=0)
    key_columns = jnp.exp(jnp.transpose(padded)[0:32])
    value_row = jnp.exp(pay_ref[0, 33:34])
    state = jnp.zeros((32, D), f32)
    for s in range(count):
        out_ref[s] = state
        weight = key_columns[:, s : s + 1] * value_row
        weight_ref[s] = weight
        state = weight * state + pay_ref[s, 0:32]


def backward_scan_kernel(count, scale, pay_ref, weight_ref, out_ref):
    state = jnp.zeros((32, D), f32)
    gain = jnp.zeros((EXTRA, D), f32)
    for s in range(count):
        gain = gain + pay_ref[s, 32:40]
    gain = gain * scale
    for s in reversed(range(count)):
        out_ref[s, 0:32] = state
        out_ref[s, 32:40] = gain
        state = weight_ref[s] * state + pay_ref[s, 0:32]


def on_device(queries, keys, values, out_grad, log_key_decay, value_rate, norm_gain):
    tokens, width = queries.shape
    heads = width // D
    blocks = tokens // BL
    around = ("outer", "inner")
    count = lax.axis_size("outer") * lax.axis_size("inner")
    head_count = lax.axis_size("head")
    rate = value_rate.reshape(heads, 1, D)
    gain = norm_gain.reshape(heads, 1, D)
    chunks = heads * 4

    turns = heads // TOGETHER

    def specs(first):
        wide = pl.BlockSpec((tokens, TOGETHER * D), lambda h: (0, h + first))
        pair = pl.BlockSpec((tokens, TOGETHER * 2 * D), lambda h: (0, h + first))
        row = pl.BlockSpec((TOGETHER, 1, D), lambda h: (h + first, 0, 0))
        eight = pl.BlockSpec((TOGETHER, blocks, D), lambda h: (h + first, 0, 0))
        square = pl.BlockSpec((TOGETHER, D, D), lambda h: (h + first, 0, 0))
        many = pl.BlockSpec((TOGETHER, blocks, D, D), lambda h: (h + first, 0, 0, 0))
        payload = pl.BlockSpec((TOGETHER * 4, 32 + EXTRA, D), lambda h: (h + first, 0, 0))
        return wide, pair, row, eight, square, many, payload

    wide, pair, row, eight, square, many, payload = specs(0)
    factors = pl.BlockSpec((tokens, 2 * D), lambda h: (0, 0))
    packed = pltpu.VMEM((TOGETHER, tokens, 2 * D), bf16)
    squares = pltpu.VMEM((TOGETHER, blocks, D, D), f32)
    sums_spec = pl.BlockSpec((head_count, 2 * blocks, D), lambda h: (0, 0, 0))

    def shape(*dims, dtype=f32):
        return jax.ShapeDtypeStruct(dims, dtype)

    wide_shape = shape(tokens, width)
    wide_low = shape(tokens, width, dtype=bf16)
    pair_shape = shape(tokens, 2 * width, dtype=bf16)
    pay_shape = shape(chunks, 32 + EXTRA, D)
    params = pltpu.CompilerParams(
        dimension_semantics=("arbitrary",), vmem_limit_bytes=VMEM_MIB * 1024 * 1024
    )

    def call(body, name, ins, outs, out_shape, scratch=(), flops=0, steps=turns, aliases={}):
        return pl.pallas_call(
            body, name=name, grid=(steps,), in_specs=ins, out_specs=outs, out_shape=out_shape,
            scratch_shapes=list(scratch), compiler_params=params, input_output_aliases=aliases,
            cost_estimate=pl.CostEstimate(
                flops=flops, transcendentals=0, bytes_accessed=16 * 1024 * 1024
            ),
        )

    pay = call(
        functools.partial(state_kernel, blocks), "state", [wide, wide, wide, row],
        payload, pay_shape,
        [pltpu.VMEM((tokens, TOGETHER * D), f32), packed, packed],
    )(keys, values, log_key_decay, rate)
    got = lax.all_to_all(pay, around, 0, 0)
    local, qd, starts, c, mid = call(
        functools.partial(local_kernel, blocks), "local",
        [wide, wide, wide, wide, row], [wide, pair, many, wide, eight],
        [
            wide_shape, pair_shape, shape(heads, blocks, D, D), wide_shape,
            shape(heads, blocks, D),
        ],
        [packed, packed, packed, packed, squares], flops=10**10,
    )(queries, keys, values, log_key_decay, rate)
    prefixes, weights = pl.pallas_call(
        functools.partial(forward_scan_kernel, count), name="fscan",
        out_shape=[shape(chunks, 32, D), shape(chunks, 32, D)],
    )(got)
    state_in = lax.all_to_all(prefixes, around, 0, 0).reshape(heads, D, D)
    core, sums = call(
        functools.partial(core_kernel, blocks, turns), "core",
        [pair, wide, wide, square, row, row], [wide, sums_spec],
        [wide_shape, shape(head_count, 2 * blocks, D)],
        [pltpu.VMEM((tokens, D), f32)] * 2,
    )(qd, local, out_grad, state_in, rate, gain)
    all_sums = lax.all_to_all(sums, "head", 0, 0)
    back_pay, factor = call(
        functools.partial(grad_kernel, blocks), "grad",
        [pair, wide, wide, sums_spec, row, row], [payload, factors],
        [pay_shape, shape(tokens, 2 * D)], [packed],
    )(qd, core, out_grad, all_sums, rate, gain)
    back_got = lax.all_to_all(back_pay, around, 0, 0)
    half = turns // 2
    made = ()
    for part in range(2):
        w, _, r, e, s, m, _ = specs(part * half)
        made = call(
            functools.partial(block_grad_kernel, blocks, len(made)), f"blockgrad{part}",
            [w, w, w, w, e, w, w, factors, m, s, r, r]
            + [pl.BlockSpec(memory_space=pl.ANY)] * len(made),
            [w, w, w], [wide_low, wide_shape, wide_shape],
            [packed] * 7 + [squares, packed], flops=10**10, steps=half,
            aliases={12 + i: i for i in range(len(made))},
        )(
            queries, keys, values, c, mid, core, out_grad, factor, starts, state_in, rate, gain,
            *made,
        )
    dq, dk_local, dv_local = made
    scale = 1.0 / math.sqrt(tokens * count)
    back_prefixes = pl.pallas_call(
        functools.partial(backward_scan_kernel, count, scale), name="bscan", out_shape=pay_shape,
    )(back_got, weights)
    back_in = lax.all_to_all(back_prefixes, around, 0, 0)
    dk, dv, gain_grad = call(
        functools.partial(final_kernel, blocks), "final",
        [wide, wide, wide, eight, wide, wide, payload, row], [wide, wide, row],
        [wide_low, wide_low, shape(heads, 1, D)],
    )(keys, values, c, mid, dk_local, dv_local, back_in, rate)
    return dq, dk, dv, gain_grad.reshape(width)


def solution(mesh):
    spec = P(("outer", "inner"), "head")
    return jax.shard_map(
        on_device,
        mesh=mesh,
        in_specs=(spec, spec, spec, spec, spec, P("head"), P("head")),
        out_specs=(spec, spec, spec, P("head")),
        check_vma=False,
    )
```

```python
import functools
import math

import jax
import jax.numpy as jnp
from jax import lax
from jax.experimental import pallas as pl
from jax.experimental.pallas import tpu as pltpu
from jax.sharding import PartitionSpec as P

HEADS = 32
D = 128
BL = 128
HALF = BL // 2
EXTRA = 8
VMEM_MIB = 56
TOGETHER = 2
f32 = jnp.float32
bf16 = jnp.bfloat16

NN = (((1,), (0,)), ((), ()))
NT = (((1,), (1,)), ((), ()))
TN = (((0,), (0,)), ((), ()))


def dot(a, b, dims):
    return lax.dot_general(a, b, dims, preferred_element_type=f32)


def pack(x):
    high = x.astype(bf16)
    return jnp.concatenate([high, (x - high.astype(f32)).astype(bf16)], axis=1)


def halves(x):
    return x[:, :D] + x[:, D:]


def nn(a, b):
    return halves(dot(a, jnp.concatenate([b, b], axis=0), NN))


def nt(a, b):
    high, low = b[:, :D], b[:, D:]
    rows_high = jnp.concatenate([high, high], axis=1)
    rows_low = jnp.concatenate([low, low], axis=1)
    return halves(dot(a, jnp.concatenate([rows_high, rows_low], axis=0), NT))


def tn(a, b):
    stacked = jnp.concatenate([a[:, :D], a[:, D:]], axis=0)
    return halves(dot(stacked, jnp.concatenate([b, b], axis=0), TN))


def tn_long(a, b):
    x = dot(a, b, TN)
    return halves(x[:D] + x[D:])


def iota(axis):
    return lax.broadcasted_iota(jnp.int32, (BL, BL), axis)


def causal():
    return iota(0) >= iota(1)


def centred_sum_matrix():
    t, s = iota(0), iota(1)
    later = ((s <= t) & (s >= HALF)).astype(f32)
    earlier = ((s > t) & (s < HALF)).astype(f32)
    return (later - earlier).astype(bf16)


def rows(b):
    return slice(b * BL, (b + 1) * BL)


def value_tables(value_log):
    steps = (iota(0) - (HALF - 1)).astype(f32) * value_log
    return jnp.exp(steps), jnp.exp(-steps)


def cols(h, width=D):
    return slice(h * width, (h + 1) * width)


def last_row(b):
    return slice((b + 1) * BL - 1, (b + 1) * BL)


def before_and_after(c_ref, mid_ref, h, blocks):
    ends = [c_ref[last_row(b), cols(h)] for b in range(blocks)]
    mids = [mid_ref[h, b : b + 1] for b in range(blocks)]
    before, total = [], jnp.zeros((1, D), f32)
    for b in range(blocks):
        before.append(total + mids[b])
        total = before[b] + ends[b]
    after, rest = [None] * blocks, jnp.zeros((1, D), f32)
    for b in reversed(range(blocks)):
        after[b] = rest + ends[b]
        rest = after[b] + mids[b]
    steps = [jnp.exp(ends[b] + mids[b + 1]) for b in range(blocks - 1)]
    return before, after, steps


def columns_of(row_list):
    stacked = jnp.concatenate(row_list, axis=0)
    padded = jnp.concatenate([stacked, jnp.zeros((D - stacked.shape[0], D), f32)], axis=0)
    return jnp.transpose(padded)


def centred_sums(blocks, ld_ref, c_ref, h):
    matrix = centred_sum_matrix()
    matrix = jnp.concatenate([matrix, matrix], axis=1)
    mids = []
    for b in range(0, blocks, 2):
        x, y = pack(ld_ref[rows(b), cols(h)]), pack(ld_ref[rows(b + 1), cols(h)])
        right = jnp.concatenate(
            [
                jnp.concatenate([x[:, :D], y[:, :D]], axis=1),
                jnp.concatenate([x[:, D:], y[:, D:]], axis=1),
            ],
            axis=0,
        )
        c = dot(matrix, right, NN)
        for at in range(2):
            c_at = c[:, cols(at)]
            c_ref[rows(b + at), cols(h)] = c_at
            first = (b + at) * BL
            mids.append(ld_ref[first : first + 1, cols(h)] - c_at[0:1])
    return mids


def state_kernel(blocks, k_ref, v_ref, ld_ref, rate_ref, pay_ref, c_s, kk, vv):
    span = blocks * BL
    all_mids = [centred_sums(blocks, ld_ref, c_s, h) for h in range(TOGETHER)]
    for h in range(TOGETHER):
        value_log = -rate_ref[h]
        _, shrink = value_tables(value_log)
        rest = jnp.zeros((1, D), f32)
        for b in reversed(range(blocks)):
            c = c_s[rows(b), cols(h)]
            after = rest + c[BL - 1 : BL]
            rest = after + all_mids[h][b]
            kk[h, rows(b)] = pack(k_ref[rows(b), cols(h)].astype(f32) * jnp.exp(after - c))
            reach = jnp.exp(value_log * float(span - BL * b - HALF))
            vv[h, rows(b)] = pack(v_ref[rows(b), cols(h)].astype(f32) * (shrink * reach))
        total = tn_long(kk[h], vv[h])
        value_total = value_log * float(span)
        for part in range(4):
            pay_ref[4 * h + part, 0:32] = total[32 * part : 32 * part + 32]
            pay_ref[4 * h + part, 32:40] = jnp.concatenate(
                [pltpu.roll(rest, (D - 32 * part) % D, 1), value_total, jnp.zeros((6, D), f32)],
                axis=0,
            )


def local_kernel(
    blocks, made, q_ref, k_ref, v_ref, ld_ref, rate_ref, *rest
):
    core_ref, qd_ref, starts_ref, c_ref, mid_ref, qs, ks, vs, scores, kv = rest[made:]
    mask = causal()
    tables = []
    for h in range(TOGETHER):
        mids = centred_sums(blocks, ld_ref, c_ref, h)
        mid_ref[h] = jnp.concatenate(mids, axis=0)
    for h in range(TOGETHER):
        grow, shrink = value_tables(-rate_ref[h])
        before, _, steps = before_and_after(c_ref, mid_ref, h, blocks)
        tables.append((grow, steps))
        for b in range(blocks):
            c = c_ref[rows(b), cols(h)]
            q = q_ref[rows(b), cols(h)].astype(f32) * jnp.exp(c)
            qs[rows(b), cols(h, 2 * D)] = pack(q)
            qd_ref[rows(b), cols(h, 2 * D)] = pack(q * jnp.exp(before[b]))
            ks[rows(b), cols(h, 2 * D)] = pack(k_ref[rows(b), cols(h)].astype(f32) * jnp.exp(-c))
            vs[rows(b), cols(h, 2 * D)] = pack(v_ref[rows(b), cols(h)].astype(f32) * shrink)
    for h in range(TOGETHER):
        for b in range(blocks):
            part = nt(qs[rows(b), cols(h, 2 * D)], ks[rows(b), cols(h, 2 * D)])
            scores[rows(b), cols(h, 2 * D)] = pack(jnp.where(mask, part, 0.0))
    for h in range(TOGETHER):
        for b in range(blocks - 1):
            kv[h, b] = tn(ks[rows(b), cols(h, 2 * D)], vs[rows(b), cols(h, 2 * D)])
    for h in range(TOGETHER):
        key_steps = columns_of(tables[h][1])
        value_step = jnp.exp(-rate_ref[h] * float(BL))
        state = jnp.zeros((D, D), f32)
        for b in range(blocks):
            starts_ref[h, b] = state
            if b < blocks - 1:
                state = (state + kv[h, b]) * (key_steps[:, b : b + 1] * value_step)
    for h in range(TOGETHER):
        for b in range(blocks):
            value, state = vs[rows(b), cols(h, 2 * D)], pack(starts_ref[h, b])
            left = jnp.concatenate([scores[rows(b), cols(h, 2 * D)], qs[rows(b), cols(h, 2 * D)]], axis=1)
            right = jnp.concatenate([value, value, state, state], axis=0)
            core_ref[rows(b), cols(h)] = tables[h][0] * halves(dot(left, right, NN))


def core_kernel(
    blocks, turns, qd_ref, local_ref, grad_ref, state_ref, rate_ref, gain_ref,
    core_ref, sums_ref, squares, crosses,
):
    turn = pl.program_id(0)

    @pl.when(turn == 0)
    def _():
        squares[...] = jnp.zeros_like(squares)
        crosses[...] = jnp.zeros_like(crosses)

    grows, rights = [], []
    for h in range(TOGETHER):
        grows.append(value_tables(-rate_ref[h])[0])
        state = pack(state_ref[h])
        rights.append(jnp.concatenate([state, state], axis=0))
    for b in range(blocks):
        square, cross = squares[rows(b)], crosses[rows(b)]
        for h in range(TOGETHER):
            reach = jnp.exp(-rate_ref[h] * float(BL * b + HALF))
            incoming = halves(dot(qd_ref[rows(b), cols(h, 2 * D)], rights[h], NN))
            core = local_ref[rows(b), cols(h)] + (grows[h] * reach) * incoming
            core_ref[rows(b), cols(h)] = core
            square = square + core * core
            cross = cross + core * (grad_ref[rows(b), cols(h)].astype(f32) * gain_ref[h])
        squares[rows(b)] = square
        crosses[rows(b)] = cross

    @pl.when(turn == turns - 1)
    def _():
        ones = jnp.ones((8, 2 * D), bf16)
        for at, ref in enumerate((squares, crosses)):
            found = [dot(ones, pack(ref[rows(b)]), NT)[0:1] for b in range(blocks)]
            all_found = jnp.concatenate(found, axis=0)
            for copy in range(sums_ref.shape[0]):
                sums_ref[copy, at * blocks : (at + 1) * blocks] = all_found


def grad_kernel(
    blocks, qd_ref, core_ref, grad_ref, sums_ref, rate_ref, gain_ref, pay_ref, factor_ref, gg
):
    turn = pl.program_id(0)
    columns = HEADS * D

    @pl.when(turn == 0)
    def _():
        both = sums_ref[0]
        for copy in range(1, sums_ref.shape[0]):
            both = both + sums_ref[copy]
        rms = lax.rsqrt(both[0:blocks] / columns + 1e-06)
        coef = rms * rms * rms * both[blocks : 2 * blocks] / columns
        for b in range(blocks):
            factor_ref[rows(b), :D] = jnp.transpose(jnp.broadcast_to(rms[b : b + 1], (BL, D)))
            factor_ref[rows(b), D:] = jnp.transpose(jnp.broadcast_to(coef[b : b + 1], (BL, D)))

    for h in range(TOGETHER):
        grow, _ = value_tables(-rate_ref[h])
        gain_sum = jnp.zeros((BL, D), f32)
        for b in range(blocks):
            core = core_ref[rows(b), cols(h)]
            out = grad_ref[rows(b), cols(h)].astype(f32) * factor_ref[rows(b), :D]
            gain_sum = gain_sum + out * core
            g = out * gain_ref[h] - core * factor_ref[rows(b), D:]
            reach = jnp.exp(-rate_ref[h] * float(BL * b + HALF))
            gg[h, rows(b)] = pack(g * (grow * reach))
        total = tn_long(qd_ref[:, cols(h, 2 * D)], gg[h])
        gain_row = jnp.sum(gain_sum, axis=0, keepdims=True)
        for part in range(4):
            pay_ref[4 * h + part, 0:32] = total[32 * part : 32 * part + 32]
            pay_ref[4 * h + part, 32:40] = jnp.concatenate(
                [gain_row, jnp.zeros((7, D), f32)], axis=0
            )


def block_grad_kernel(
    blocks, made, qs, ks, vs, scores, c_ref, mid_ref, core_ref, grad_ref, factor_ref,
    starts_ref, state_ref, rate_ref, gain_ref, *rest,
):
    dq_ref, dk_ref, dv_ref, gs, start, mixed, qg, passed = rest[made:]
    mask = causal()
    tables = []
    for h in range(TOGETHER):
        grow, shrink = value_tables(-rate_ref[h])
        before, _, steps = before_and_after(c_ref, mid_ref, h, blocks)
        key_columns = columns_of(steps + [jnp.exp(x) for x in before])
        tables.append((shrink, key_columns))
        for b in range(blocks):
            out = grad_ref[rows(b), cols(h)].astype(f32) * factor_ref[rows(b), :D]
            g = out * gain_ref[h] - core_ref[rows(b), cols(h)] * factor_ref[rows(b), D:]
            gs[h, rows(b)] = pack(g * grow)
            at = blocks - 1 + b
            reach = jnp.exp(-rate_ref[h] * float(BL * b + HALF))
            begun = starts_ref[h, b] + state_ref[h] * (key_columns[:, at : at + 1] * reach)
            start[h, rows(b)] = pack(begun)
    for h in range(TOGETHER):
        for b in range(blocks):
            part = nt(gs[h, rows(b)], vs[rows(b), cols(h, 2 * D)])
            mixed[h, rows(b)] = pack(jnp.where(mask, part, 0.0))
    for h in range(TOGETHER):
        for b in range(1, blocks):
            qg[h, b] = tn(qs[rows(b), cols(h, 2 * D)], gs[h, rows(b)])
    for h in range(TOGETHER):
        value_step = jnp.exp(-rate_ref[h] * float(BL))
        now = jnp.zeros((D, D), f32)
        for b in reversed(range(blocks)):
            passed[h, rows(b)] = pack(now)
            if b:
                now = (now + qg[h, b]) * (tables[h][1][:, b - 1 : b] * value_step)
    for h in range(TOGETHER):
        for b in range(blocks):
            dq = nn(mixed[h, rows(b)], ks[rows(b), cols(h, 2 * D)]) + nt(gs[h, rows(b)], start[h, rows(b)])
            dq_ref[rows(b), cols(h)] = (jnp.exp(c_ref[rows(b), cols(h)]) * dq).astype(bf16)
    for h in range(TOGETHER):
        for b in range(blocks):
            dk = tn(mixed[h, rows(b)], qs[rows(b), cols(h, 2 * D)]) + nt(vs[rows(b), cols(h, 2 * D)], passed[h, rows(b)])
            dk_ref[rows(b), cols(h)] = jnp.exp(-c_ref[rows(b), cols(h)]) * dk
    for h in range(TOGETHER):
        for b in range(blocks):
            dv = tn(scores[rows(b), cols(h, 2 * D)], gs[h, rows(b)]) + nn(ks[rows(b), cols(h, 2 * D)], passed[h, rows(b)])
            dv_ref[rows(b), cols(h)] = tables[h][0] * dv


def final_kernel(
    blocks, k_ref, v_ref, c_ref, mid_ref, dk_ref, dv_ref, back_ref, rate_ref,
    dk_out, dv_out, gain_out,
):
    span = blocks * BL
    for h in range(TOGETHER):
        value_log = -rate_ref[h]
        _, shrink = value_tables(value_log)
        _, after, _ = before_and_after(c_ref, mid_ref, h, blocks)
        back = pack(back_ref[4 * h : 4 * h + 4, 0:32].reshape(D, D))
        for b in range(blocks):
            at = rows(b), cols(h)
            fade = jnp.exp(after[b] - c_ref[at])
            value_fade = shrink * jnp.exp(value_log * float(span - BL * b - HALF))
            ks = pack(k_ref[at].astype(f32) * fade)
            vs = pack(v_ref[at].astype(f32) * value_fade)
            dk_out[at] = (dk_ref[at] + fade * nt(vs, back)).astype(bf16)
            dv_out[at] = (dv_ref[at] + value_fade * nn(ks, back)).astype(bf16)
        gain_out[h] = back_ref[4 * h, 32:33]


def key_weights(count, extra_ref):
    decays = jnp.concatenate([extra_ref[s, 0:1] for s in range(count)], axis=0)
    padded = jnp.concatenate([decays, jnp.zeros((D - count, D), f32)], axis=0)
    return jnp.exp(jnp.transpose(padded)[0:32]), jnp.exp(extra_ref[0, 1:2])


def forward_scan_kernel(count, pay_ref, extra_ref, out_ref):
    key_columns, value_row = key_weights(count, extra_ref)
    state = jnp.zeros((32, D), f32)
    for s in range(count):
        out_ref[s] = state
        state = (key_columns[:, s : s + 1] * value_row) * state + pay_ref[s]


def backward_scan_kernel(count, scale, pay_ref, gain_ref, extra_ref, out_ref):
    key_columns, value_row = key_weights(count, extra_ref)
    state = jnp.zeros((32, D), f32)
    gain = jnp.zeros((EXTRA, D), f32)
    for s in range(count):
        gain = gain + gain_ref[s]
    gain = gain * scale
    for s in reversed(range(count)):
        out_ref[s, 0:32] = state
        out_ref[s, 32:40] = gain
        state = (key_columns[:, s : s + 1] * value_row) * state + pay_ref[s]


def on_device(queries, keys, values, out_grad, log_key_decay, value_rate, norm_gain):
    tokens, width = queries.shape
    heads = width // D
    blocks = tokens // BL
    around = ("outer", "inner")
    count = lax.axis_size("outer") * lax.axis_size("inner")
    head_count = lax.axis_size("head")
    rate = value_rate.reshape(heads, 1, D)
    gain = norm_gain.reshape(heads, 1, D)
    chunks = heads * 4

    turns = heads // TOGETHER

    def specs(first):
        wide = pl.BlockSpec((tokens, TOGETHER * D), lambda h: (0, h + first))
        pair = pl.BlockSpec((tokens, TOGETHER * 2 * D), lambda h: (0, h + first))
        row = pl.BlockSpec((TOGETHER, 1, D), lambda h: (h + first, 0, 0))
        eight = pl.BlockSpec((TOGETHER, blocks, D), lambda h: (h + first, 0, 0))
        square = pl.BlockSpec((TOGETHER, D, D), lambda h: (h + first, 0, 0))
        many = pl.BlockSpec((TOGETHER, blocks, D, D), lambda h: (h + first, 0, 0, 0))
        payload = pl.BlockSpec((TOGETHER * 4, 32 + EXTRA, D), lambda h: (h + first, 0, 0))
        return wide, pair, row, eight, square, many, payload

    wide, pair, row, eight, square, many, payload = specs(0)
    factors = pl.BlockSpec((tokens, 2 * D), lambda h: (0, 0))
    packed = pltpu.VMEM((TOGETHER, tokens, 2 * D), bf16)
    squares = pltpu.VMEM((TOGETHER, blocks, D, D), f32)
    sums_spec = pl.BlockSpec((head_count, 2 * blocks, D), lambda h: (0, 0, 0))

    def shape(*dims, dtype=f32):
        return jax.ShapeDtypeStruct(dims, dtype)

    wide_shape = shape(tokens, width)
    wide_low = shape(tokens, width, dtype=bf16)
    pair_shape = shape(tokens, 2 * width, dtype=bf16)
    pay_shape = shape(chunks, 32 + EXTRA, D)
    def hbm(*arrays):
        return [pltpu.with_memory_space_constraint(x, pltpu.HBM) for x in arrays]

    def call(body, name, ins, outs, out_shape, scratch=(), flops=0, steps=turns, aliases={}, limit=VMEM_MIB):
        return pl.pallas_call(
            body, name=name, grid=(steps,), in_specs=ins, out_specs=outs, out_shape=out_shape,
            scratch_shapes=list(scratch), input_output_aliases=aliases,
            compiler_params=pltpu.CompilerParams(
                dimension_semantics=("arbitrary",), vmem_limit_bytes=limit * 1024 * 1024
            ),
            cost_estimate=pl.CostEstimate(
                flops=flops, transcendentals=0, bytes_accessed=16 * 1024 * 1024
            ),
        )

    pay = call(
        functools.partial(state_kernel, blocks), "state", [wide, wide, wide, row],
        payload, pay_shape,
        [pltpu.VMEM((tokens, TOGETHER * D), f32), packed, packed],
    )(keys, values, log_key_decay, rate)
    got = lax.all_to_all(pay, around, 0, 0)
    half = turns // 2
    made = ()
    for part in range(2):
        w, p, r, e, s, m, _ = specs(part * half)
        made = call(
            functools.partial(local_kernel, blocks, len(made)), f"local{part}",
            [w, w, w, w, r] + [pl.BlockSpec(memory_space=pl.ANY)] * len(made),
            [w, p, m, w, e, p, p, p, p],
            [
                wide_shape, pair_shape, shape(heads, blocks, D, D), wide_shape,
                shape(heads, blocks, D), pair_shape, pair_shape, pair_shape, pair_shape,
            ],
            [squares], flops=10**10, steps=half, aliases={5 + i: i for i in range(len(made))},
        )(queries, keys, values, log_key_decay, rate, *made)
    local, qd, starts, c, mid, qs, ks, vs, scores = made
    top = pl.BlockSpec((count, 32, D), lambda i: (0, 0, 0))
    bottom = pl.BlockSpec((count, EXTRA, D), lambda i: (0, 32 // EXTRA, 0))
    full = pl.BlockSpec((count, 32 + EXTRA, D), lambda i: (0, 0, 0))
    small = pltpu.CompilerParams(
        dimension_semantics=("arbitrary",), vmem_limit_bytes=8 * 1024 * 1024
    )
    prefixes = pl.pallas_call(
        functools.partial(forward_scan_kernel, count), name="fscan", grid=(1,),
        in_specs=[top, bottom], out_specs=top, out_shape=shape(chunks, 32, D),
        compiler_params=small,
    )(got, got)
    state_in = lax.all_to_all(prefixes, around, 0, 0).reshape(heads, D, D)
    core, sums = call(
        functools.partial(core_kernel, blocks, turns), "core",
        [pair, wide, wide, square, row, row], [wide, sums_spec],
        [pltpu.HBM(wide_shape.shape, f32), shape(head_count, 2 * blocks, D)],
        [pltpu.VMEM((tokens, D), f32)] * 2, limit=24,
    )(*hbm(qd, local, out_grad), state_in, rate, gain)
    all_sums = lax.all_to_all(sums, "head", 0, 0)
    back_pay, factor = call(
        functools.partial(grad_kernel, blocks), "grad",
        [pair, wide, wide, sums_spec, row, row], [payload, factors],
        [pay_shape, shape(tokens, 2 * D)], [packed],
    )(qd, core, out_grad, all_sums, rate, gain)
    back_got = lax.all_to_all(back_pay, around, 0, 0)
    made = ()
    for part in range(2):
        w, p, r, e, s, m, _ = specs(part * half)
        made = call(
            functools.partial(block_grad_kernel, blocks, len(made)), f"blockgrad{part}",
            [p, p, p, p, w, e, w, w, factors, m, s, r, r]
            + [pl.BlockSpec(memory_space=pl.ANY)] * len(made),
            [w, w, w], [wide_low, wide_shape, wide_shape],
            [packed] * 3 + [squares, packed], flops=10**10, steps=half,
            aliases={13 + i: i for i in range(len(made))},
        )(
            qs, ks, vs, scores, c, mid, core, out_grad, factor, starts, state_in, rate, gain,
            *made,
        )
    dq, dk_local, dv_local = made
    scale = 1.0 / math.sqrt(tokens * count)
    back_prefixes = pl.pallas_call(
        functools.partial(backward_scan_kernel, count, scale), name="bscan", grid=(1,),
        in_specs=[top, bottom, bottom], out_specs=full, out_shape=pay_shape,
        compiler_params=small,
    )(back_got, back_got, got)
    back_in = lax.all_to_all(back_prefixes, around, 0, 0)
    dk, dv, gain_grad = call(
        functools.partial(final_kernel, blocks), "final",
        [wide, wide, wide, eight, wide, wide, payload, row], [wide, wide, row],
        [wide_low, wide_low, shape(heads, 1, D)], limit=24,
    )(*hbm(keys, values, c), mid, *hbm(dk_local, dv_local), back_in, rate)
    return dq, dk, dv, gain_grad.reshape(width)


def solution(mesh):
    spec = P(("outer", "inner"), "head")
    return jax.shard_map(
        on_device,
        mesh=mesh,
        in_specs=(spec, spec, spec, spec, spec, P("head"), P("head")),
        out_specs=(spec, spec, spec, P("head")),
        check_vma=False,
    )
```

```python
import functools
import math

import jax
import jax.numpy as jnp
from jax import lax
from jax.experimental import pallas as pl
from jax.experimental.pallas import tpu as pltpu
from jax.sharding import PartitionSpec as P

HEADS = 32
D = 128
BL = 128
HALF = BL // 2
EXTRA = 8
VMEM_MIB = 56
TOGETHER = 2
f32 = jnp.float32
bf16 = jnp.bfloat16

NN = (((1,), (0,)), ((), ()))
NT = (((1,), (1,)), ((), ()))
TN = (((0,), (0,)), ((), ()))


def dot(a, b, dims):
    return lax.dot_general(a, b, dims, preferred_element_type=f32)


def pack(x):
    high = x.astype(bf16)
    return jnp.concatenate([high, (x - high.astype(f32)).astype(bf16)], axis=1)


def halves(x):
    return x[:, :D] + x[:, D:]


def nn(a, b):
    return halves(dot(a, jnp.concatenate([b, b], axis=0), NN))


def nt(a, b):
    high, low = b[:, :D], b[:, D:]
    rows_high = jnp.concatenate([high, high], axis=1)
    rows_low = jnp.concatenate([low, low], axis=1)
    return halves(dot(a, jnp.concatenate([rows_high, rows_low], axis=0), NT))


def tn(a, b):
    stacked = jnp.concatenate([a[:, :D], a[:, D:]], axis=0)
    return halves(dot(stacked, jnp.concatenate([b, b], axis=0), TN))


def tn_long(a, b):
    x = dot(a, b, TN)
    return halves(x[:D] + x[D:])


def iota(axis):
    return lax.broadcasted_iota(jnp.int32, (BL, BL), axis)


def causal():
    return iota(0) >= iota(1)


def centred_sum_matrix():
    t, s = iota(0), iota(1)
    later = ((s <= t) & (s >= HALF)).astype(f32)
    earlier = ((s > t) & (s < HALF)).astype(f32)
    return (later - earlier).astype(bf16)


def rows(b):
    return slice(b * BL, (b + 1) * BL)


def value_tables(value_log):
    steps = (iota(0) - (HALF - 1)).astype(f32) * value_log
    return jnp.exp(steps), jnp.exp(-steps)


def cols(h, width=D):
    return slice(h * width, (h + 1) * width)


def last_row(b):
    return slice((b + 1) * BL - 1, (b + 1) * BL)


def before_and_after(c_ref, mid_ref, h, blocks):
    ends = [c_ref[last_row(b), cols(h)] for b in range(blocks)]
    mids = [mid_ref[h, b : b + 1] for b in range(blocks)]
    before, total = [], jnp.zeros((1, D), f32)
    for b in range(blocks):
        before.append(total + mids[b])
        total = before[b] + ends[b]
    after, rest = [None] * blocks, jnp.zeros((1, D), f32)
    for b in reversed(range(blocks)):
        after[b] = rest + ends[b]
        rest = after[b] + mids[b]
    steps = [jnp.exp(ends[b] + mids[b + 1]) for b in range(blocks - 1)]
    return before, after, steps


def columns_of(row_list):
    stacked = jnp.concatenate(row_list, axis=0)
    padded = jnp.concatenate([stacked, jnp.zeros((D - stacked.shape[0], D), f32)], axis=0)
    return jnp.transpose(padded)


def centred_sums(blocks, ld_ref, c_ref, h):
    matrix = centred_sum_matrix()
    matrix = jnp.concatenate([matrix, matrix], axis=1)
    mids = []
    for b in range(0, blocks, 2):
        x, y = pack(ld_ref[rows(b), cols(h)]), pack(ld_ref[rows(b + 1), cols(h)])
        right = jnp.concatenate(
            [
                jnp.concatenate([x[:, :D], y[:, :D]], axis=1),
                jnp.concatenate([x[:, D:], y[:, D:]], axis=1),
            ],
            axis=0,
        )
        c = dot(matrix, right, NN)
        for at in range(2):
            c_at = c[:, cols(at)]
            c_ref[rows(b + at), cols(h)] = c_at
            first = (b + at) * BL
            mids.append(ld_ref[first : first + 1, cols(h)] - c_at[0:1])
    return mids


def state_kernel(blocks, k_ref, v_ref, ld_ref, rate_ref, pay_ref, c_s, kk, vv):
    span = blocks * BL
    all_mids = [centred_sums(blocks, ld_ref, c_s, h) for h in range(TOGETHER)]
    for h in range(TOGETHER):
        value_log = -rate_ref[h]
        _, shrink = value_tables(value_log)
        rest = jnp.zeros((1, D), f32)
        for b in reversed(range(blocks)):
            c = c_s[rows(b), cols(h)]
            after = rest + c[BL - 1 : BL]
            rest = after + all_mids[h][b]
            kk[h, rows(b)] = pack(k_ref[rows(b), cols(h)].astype(f32) * jnp.exp(after - c))
            reach = jnp.exp(value_log * float(span - BL * b - HALF))
            vv[h, rows(b)] = pack(v_ref[rows(b), cols(h)].astype(f32) * (shrink * reach))
        total = tn_long(kk[h], vv[h])
        value_total = value_log * float(span)
        for part in range(4):
            pay_ref[4 * h + part, 0:32] = total[32 * part : 32 * part + 32]
            pay_ref[4 * h + part, 32:40] = jnp.concatenate(
                [pltpu.roll(rest, (D - 32 * part) % D, 1), value_total, jnp.zeros((6, D), f32)],
                axis=0,
            )


def local_kernel(
    blocks, made, q_ref, k_ref, v_ref, ld_ref, rate_ref, *rest
):
    core_ref, qd_ref, starts_ref, c_ref, mid_ref, qs, ks, vs, scores, kv = rest[made:]
    mask = causal()
    tables = []
    for h in range(TOGETHER):
        mids = centred_sums(blocks, ld_ref, c_ref, h)
        mid_ref[h] = jnp.concatenate(mids, axis=0)
    for h in range(TOGETHER):
        grow, shrink = value_tables(-rate_ref[h])
        before, _, steps = before_and_after(c_ref, mid_ref, h, blocks)
        tables.append((grow, steps))
        for b in range(blocks):
            c = c_ref[rows(b), cols(h)]
            q = q_ref[rows(b), cols(h)].astype(f32) * jnp.exp(c)
            qs[rows(b), cols(h, 2 * D)] = pack(q)
            qd_ref[rows(b), cols(h, 2 * D)] = pack(q * jnp.exp(before[b]))
            ks[rows(b), cols(h, 2 * D)] = pack(k_ref[rows(b), cols(h)].astype(f32) * jnp.exp(-c))
            vs[rows(b), cols(h, 2 * D)] = pack(v_ref[rows(b), cols(h)].astype(f32) * shrink)
    for h in range(TOGETHER):
        for b in range(blocks):
            part = nt(qs[rows(b), cols(h, 2 * D)], ks[rows(b), cols(h, 2 * D)])
            scores[rows(b), cols(h, 2 * D)] = pack(jnp.where(mask, part, 0.0))
    for h in range(TOGETHER):
        for b in range(blocks - 1):
            kv[h, b] = tn(ks[rows(b), cols(h, 2 * D)], vs[rows(b), cols(h, 2 * D)])
    for h in range(TOGETHER):
        key_steps = columns_of(tables[h][1])
        value_step = jnp.exp(-rate_ref[h] * float(BL))
        state = jnp.zeros((D, D), f32)
        for b in range(blocks):
            starts_ref[h, b] = state
            if b < blocks - 1:
                state = (state + kv[h, b]) * (key_steps[:, b : b + 1] * value_step)
    for h in range(TOGETHER):
        for b in range(blocks):
            value, state = vs[rows(b), cols(h, 2 * D)], pack(starts_ref[h, b])
            left = jnp.concatenate([scores[rows(b), cols(h, 2 * D)], qs[rows(b), cols(h, 2 * D)]], axis=1)
            right = jnp.concatenate([value, value, state, state], axis=0)
            core_ref[rows(b), cols(h)] = tables[h][0] * halves(dot(left, right, NN))


def core_kernel(
    blocks, turns, qd_ref, local_ref, grad_ref, state_ref, rate_ref, gain_ref,
    near_ref, near_qd_ref, near_grad_ref, sums_ref, squares, crosses,
):
    turn = pl.program_id(0)
    near_qd_ref[...] = qd_ref[...]
    near_grad_ref[...] = grad_ref[...]

    @pl.when(turn == 0)
    def _():
        squares[...] = jnp.zeros_like(squares)
        crosses[...] = jnp.zeros_like(crosses)

    grows, rights = [], []
    for h in range(TOGETHER):
        grows.append(value_tables(-rate_ref[h])[0])
        state = pack(state_ref[h])
        rights.append(jnp.concatenate([state, state], axis=0))
    for b in range(blocks):
        square, cross = squares[rows(b)], crosses[rows(b)]
        for h in range(TOGETHER):
            reach = jnp.exp(-rate_ref[h] * float(BL * b + HALF))
            incoming = halves(dot(qd_ref[rows(b), cols(h, 2 * D)], rights[h], NN))
            core = local_ref[rows(b), cols(h)] + (grows[h] * reach) * incoming
            near_ref[rows(b), cols(h)] = core
            square = square + core * core
            cross = cross + core * (grad_ref[rows(b), cols(h)].astype(f32) * gain_ref[h])
        squares[rows(b)] = square
        crosses[rows(b)] = cross

    @pl.when(turn == turns - 1)
    def _():
        ones = jnp.ones((8, 2 * D), bf16)
        for at, ref in enumerate((squares, crosses)):
            found = [dot(ones, pack(ref[rows(b)]), NT)[0:1] for b in range(blocks)]
            all_found = jnp.concatenate(found, axis=0)
            for copy in range(sums_ref.shape[0]):
                sums_ref[copy, at * blocks : (at + 1) * blocks] = all_found


def grad_kernel(
    blocks, qd_ref, core_ref, grad_ref, rate_ref, gain_ref, *rest
):
    *sums_refs, pay_ref, factor_ref, kept_ref, gg = rest
    turn = pl.program_id(0)
    columns = HEADS * D

    @pl.when(turn == 0)
    def _():
        both = sums_refs[0][0]
        for ref in sums_refs[1:]:
            both = both + ref[0]
        rms = lax.rsqrt(both[0:blocks] / columns + 1e-06)
        coef = rms * rms * rms * both[blocks : 2 * blocks] / columns
        for b in range(blocks):
            factor_ref[rows(b), :D] = jnp.transpose(jnp.broadcast_to(rms[b : b + 1], (BL, D)))
            factor_ref[rows(b), D:] = jnp.transpose(jnp.broadcast_to(coef[b : b + 1], (BL, D)))

    for h in range(TOGETHER):
        grow, _ = value_tables(-rate_ref[h])
        gain_sum = jnp.zeros((BL, D), f32)
        for b in range(blocks):
            core = core_ref[rows(b), cols(h)]
            kept_ref[rows(b), cols(h)] = core
            out = grad_ref[rows(b), cols(h)].astype(f32) * factor_ref[rows(b), :D]
            gain_sum = gain_sum + out * core
            g = out * gain_ref[h] - core * factor_ref[rows(b), D:]
            reach = jnp.exp(-rate_ref[h] * float(BL * b + HALF))
            gg[h, rows(b)] = pack(g * (grow * reach))
        total = tn_long(qd_ref[:, cols(h, 2 * D)], gg[h])
        gain_row = jnp.sum(gain_sum, axis=0, keepdims=True)
        for part in range(4):
            pay_ref[4 * h + part, 0:32] = total[32 * part : 32 * part + 32]
            pay_ref[4 * h + part, 32:40] = jnp.concatenate(
                [gain_row, jnp.zeros((7, D), f32)], axis=0
            )


def block_grad_kernel(
    blocks, made, qs, ks, vs, scores, c_ref, mid_ref, core_ref, grad_ref, factor_ref,
    starts_ref, state_ref, rate_ref, gain_ref, *rest,
):
    dq_ref, dk_ref, dv_ref, gs, start, mixed, qg, passed = rest[made:]
    mask = causal()
    tables = []
    for h in range(TOGETHER):
        grow, shrink = value_tables(-rate_ref[h])
        before, _, steps = before_and_after(c_ref, mid_ref, h, blocks)
        key_columns = columns_of(steps + [jnp.exp(x) for x in before])
        tables.append((shrink, key_columns))
        for b in range(blocks):
            out = grad_ref[rows(b), cols(h)].astype(f32) * factor_ref[rows(b), :D]
            g = out * gain_ref[h] - core_ref[rows(b), cols(h)] * factor_ref[rows(b), D:]
            gs[h, rows(b)] = pack(g * grow)
            at = blocks - 1 + b
            reach = jnp.exp(-rate_ref[h] * float(BL * b + HALF))
            begun = starts_ref[h, b] + state_ref[h] * (key_columns[:, at : at + 1] * reach)
            start[h, rows(b)] = pack(begun)
    for h in range(TOGETHER):
        for b in range(blocks):
            part = nt(gs[h, rows(b)], vs[rows(b), cols(h, 2 * D)])
            mixed[h, rows(b)] = pack(jnp.where(mask, part, 0.0))
    for h in range(TOGETHER):
        for b in range(1, blocks):
            qg[h, b] = tn(qs[rows(b), cols(h, 2 * D)], gs[h, rows(b)])
    for h in range(TOGETHER):
        value_step = jnp.exp(-rate_ref[h] * float(BL))
        now = jnp.zeros((D, D), f32)
        for b in reversed(range(blocks)):
            passed[h, rows(b)] = pack(now)
            if b:
                now = (now + qg[h, b]) * (tables[h][1][:, b - 1 : b] * value_step)
    for h in range(TOGETHER):
        for b in range(blocks):
            dq = nn(mixed[h, rows(b)], ks[rows(b), cols(h, 2 * D)]) + nt(gs[h, rows(b)], start[h, rows(b)])
            dq_ref[rows(b), cols(h)] = (jnp.exp(c_ref[rows(b), cols(h)]) * dq).astype(bf16)
    for h in range(TOGETHER):
        for b in range(blocks):
            dk = tn(mixed[h, rows(b)], qs[rows(b), cols(h, 2 * D)]) + nt(vs[rows(b), cols(h, 2 * D)], passed[h, rows(b)])
            dk_ref[rows(b), cols(h)] = jnp.exp(-c_ref[rows(b), cols(h)]) * dk
    for h in range(TOGETHER):
        for b in range(blocks):
            dv = tn(scores[rows(b), cols(h, 2 * D)], gs[h, rows(b)]) + nn(ks[rows(b), cols(h, 2 * D)], passed[h, rows(b)])
            dv_ref[rows(b), cols(h)] = tables[h][0] * dv


def final_kernel(
    blocks, k_ref, v_ref, c_ref, mid_ref, dk_ref, dv_ref, back_ref, rate_ref,
    dk_out, dv_out, gain_out,
):
    span = blocks * BL
    for h in range(TOGETHER):
        value_log = -rate_ref[h]
        _, shrink = value_tables(value_log)
        _, after, _ = before_and_after(c_ref, mid_ref, h, blocks)
        back = pack(back_ref[4 * h : 4 * h + 4, 0:32].reshape(D, D))
        for b in range(blocks):
            at = rows(b), cols(h)
            fade = jnp.exp(after[b] - c_ref[at])
            value_fade = shrink * jnp.exp(value_log * float(span - BL * b - HALF))
            ks = pack(k_ref[at].astype(f32) * fade)
            vs = pack(v_ref[at].astype(f32) * value_fade)
            dk_out[at] = (dk_ref[at] + fade * nt(vs, back)).astype(bf16)
            dv_out[at] = (dv_ref[at] + value_fade * nn(ks, back)).astype(bf16)
        gain_out[h] = back_ref[4 * h, 32:33]


def key_weights(count, extra_ref):
    decays = jnp.concatenate([extra_ref[s, 0:1] for s in range(count)], axis=0)
    padded = jnp.concatenate([decays, jnp.zeros((D - count, D), f32)], axis=0)
    return jnp.exp(jnp.transpose(padded)[0:32]), jnp.exp(extra_ref[0, 1:2])


def forward_scan_kernel(count, pay_ref, extra_ref, out_ref):
    key_columns, value_row = key_weights(count, extra_ref)
    state = jnp.zeros((32, D), f32)
    for s in range(count):
        out_ref[s] = state
        state = (key_columns[:, s : s + 1] * value_row) * state + pay_ref[s]


def backward_scan_kernel(count, scale, pay_ref, gain_ref, extra_ref, out_ref):
    key_columns, value_row = key_weights(count, extra_ref)
    state = jnp.zeros((32, D), f32)
    gain = jnp.zeros((EXTRA, D), f32)
    for s in range(count):
        gain = gain + gain_ref[s]
    gain = gain * scale
    for s in reversed(range(count)):
        out_ref[s, 0:32] = state
        out_ref[s, 32:40] = gain
        state = (key_columns[:, s : s + 1] * value_row) * state + pay_ref[s]


def on_device(queries, keys, values, out_grad, log_key_decay, value_rate, norm_gain):
    tokens, width = queries.shape
    heads = width // D
    blocks = tokens // BL
    around = ("outer", "inner")
    count = lax.axis_size("outer") * lax.axis_size("inner")
    head_count = lax.axis_size("head")
    rate = value_rate.reshape(heads, 1, D)
    gain = norm_gain.reshape(heads, 1, D)
    chunks = heads * 4

    turns = heads // TOGETHER

    def specs(first):
        wide = pl.BlockSpec((tokens, TOGETHER * D), lambda h: (0, h + first))
        pair = pl.BlockSpec((tokens, TOGETHER * 2 * D), lambda h: (0, h + first))
        row = pl.BlockSpec((TOGETHER, 1, D), lambda h: (h + first, 0, 0))
        eight = pl.BlockSpec((TOGETHER, blocks, D), lambda h: (h + first, 0, 0))
        square = pl.BlockSpec((TOGETHER, D, D), lambda h: (h + first, 0, 0))
        many = pl.BlockSpec((TOGETHER, blocks, D, D), lambda h: (h + first, 0, 0, 0))
        payload = pl.BlockSpec((TOGETHER * 4, 32 + EXTRA, D), lambda h: (h + first, 0, 0))
        return wide, pair, row, eight, square, many, payload

    wide, pair, row, eight, square, many, payload = specs(0)
    factors = pl.BlockSpec((tokens, 2 * D), lambda h: (0, 0))
    packed = pltpu.VMEM((TOGETHER, tokens, 2 * D), bf16)
    squares = pltpu.VMEM((TOGETHER, blocks, D, D), f32)
    sums_spec = pl.BlockSpec((1, 2 * blocks, D), lambda h: (0, 0, 0))

    def shape(*dims, dtype=f32):
        return jax.ShapeDtypeStruct(dims, dtype)

    wide_shape = shape(tokens, width)
    wide_low = shape(tokens, width, dtype=bf16)
    pair_shape = shape(tokens, 2 * width, dtype=bf16)
    pay_shape = shape(chunks, 32 + EXTRA, D)
    def hbm(*arrays):
        return [pltpu.with_memory_space_constraint(x, pltpu.HBM) for x in arrays]

    def call(body, name, ins, outs, out_shape, scratch=(), flops=0, steps=turns, aliases={}, limit=VMEM_MIB):
        return pl.pallas_call(
            body, name=name, grid=(steps,), in_specs=ins, out_specs=outs, out_shape=out_shape,
            scratch_shapes=list(scratch), input_output_aliases=aliases,
            compiler_params=pltpu.CompilerParams(
                dimension_semantics=("arbitrary",), vmem_limit_bytes=limit * 1024 * 1024
            ),
            cost_estimate=pl.CostEstimate(
                flops=flops, transcendentals=0, bytes_accessed=16 * 1024 * 1024
            ),
        )

    pay = call(
        functools.partial(state_kernel, blocks), "state", [wide, wide, wide, row],
        payload, pay_shape,
        [pltpu.VMEM((tokens, TOGETHER * D), f32), packed, packed],
    )(keys, values, log_key_decay, rate)
    got = lax.all_to_all(pay, around, 0, 0)
    half = turns // 2
    made = ()
    for part in range(2):
        w, p, r, e, s, m, _ = specs(part * half)
        made = call(
            functools.partial(local_kernel, blocks, len(made)), f"local{part}",
            [w, w, w, w, r] + [pl.BlockSpec(memory_space=pl.ANY)] * len(made),
            [w, p, m, w, e, p, p, p, p],
            [
                wide_shape, pair_shape, shape(heads, blocks, D, D), wide_shape,
                shape(heads, blocks, D), pair_shape, pair_shape, pair_shape, pair_shape,
            ],
            [squares], flops=10**10, steps=half, aliases={5 + i: i for i in range(len(made))},
        )(queries, keys, values, log_key_decay, rate, *made)
    local, qd, starts, c, mid, qs, ks, vs, scores = made
    top = pl.BlockSpec((count, 32, D), lambda i: (0, 0, 0))
    bottom = pl.BlockSpec((count, EXTRA, D), lambda i: (0, 32 // EXTRA, 0))
    full = pl.BlockSpec((count, 32 + EXTRA, D), lambda i: (0, 0, 0))
    small = pltpu.CompilerParams(
        dimension_semantics=("arbitrary",), vmem_limit_bytes=8 * 1024 * 1024
    )
    prefixes = pl.pallas_call(
        functools.partial(forward_scan_kernel, count), name="fscan", grid=(1,),
        in_specs=[top, bottom], out_specs=top, out_shape=shape(chunks, 32, D),
        compiler_params=small,
    )(got, got)
    state_in = lax.all_to_all(prefixes, around, 0, 0).reshape(heads, D, D)
    near, near_qd, near_grad, sums = call(
        functools.partial(core_kernel, blocks, turns), "core",
        [pair, wide, wide, square, row, row], [wide, pair, wide, sums_spec],
        [
            wide_shape, pair_shape, wide_low, shape(1, 2 * blocks, D),
        ],
        [pltpu.VMEM((tokens, D), f32)] * 2, limit=24,
    )(*hbm(qd, local, out_grad), state_in, rate, gain)
    all_sums = [sums] + [
        lax.ppermute(sums, "head", [(i, i ^ step) for i in range(head_count)])
        for step in (2, 1, 3)
    ]
    back_pay, factor, core = call(
        functools.partial(grad_kernel, blocks), "grad",
        [pair, wide, wide, row, row] + [sums_spec] * head_count, [payload, factors, wide],
        [pay_shape, pltpu.HBM((tokens, 2 * D), f32), pltpu.HBM(wide_shape.shape, f32)],
        [packed], limit=24,
    )(near_qd, near, near_grad, rate, gain, *all_sums)
    back_got = lax.all_to_all(back_pay, around, 0, 0)
    made = ()
    for part in range(2):
        w, p, r, e, s, m, _ = specs(part * half)
        made = call(
            functools.partial(block_grad_kernel, blocks, len(made)), f"blockgrad{part}",
            [p, p, p, p, w, e, w, w, factors, m, s, r, r]
            + [pl.BlockSpec(memory_space=pl.ANY)] * len(made),
            [w, w, w], [wide_low, wide_shape, wide_shape],
            [packed] * 3 + [squares, packed], flops=10**10, steps=half,
            aliases={13 + i: i for i in range(len(made))},
        )(
            qs, ks, vs, scores, c, mid, core, out_grad, factor, starts, state_in, rate, gain,
            *made,
        )
    dq, dk_local, dv_local = made
    scale = 1.0 / math.sqrt(tokens * count)
    back_prefixes = pl.pallas_call(
        functools.partial(backward_scan_kernel, count, scale), name="bscan", grid=(1,),
        in_specs=[top, bottom, bottom], out_specs=full, out_shape=pay_shape,
        compiler_params=small,
    )(back_got, back_got, got)
    back_in = lax.all_to_all(back_prefixes, around, 0, 0)
    dk, dv, gain_grad = call(
        functools.partial(final_kernel, blocks), "final",
        [wide, wide, wide, eight, wide, wide, payload, row], [wide, wide, row],
        [wide_low, wide_low, shape(heads, 1, D)], limit=24,
    )(*hbm(keys, values, c), mid, *hbm(dk_local, dv_local), back_in, rate)
    return dq, dk, dv, gain_grad.reshape(width)


def solution(mesh):
    spec = P(("outer", "inner"), "head")
    return jax.shard_map(
        on_device,
        mesh=mesh,
        in_specs=(spec, spec, spec, spec, spec, P("head"), P("head")),
        out_specs=(spec, spec, spec, P("head")),
        check_vma=False,
    )
```

```python
import functools
import math

import jax
import jax.numpy as jnp
from jax import lax
from jax.experimental import pallas as pl
from jax.experimental.pallas import tpu as pltpu
from jax.sharding import PartitionSpec as P

HEADS = 32
D = 128
BL = 128
HALF = BL // 2
EXTRA = 8
VMEM_MIB = 56
TOGETHER = 2
f32 = jnp.float32
bf16 = jnp.bfloat16

NN = (((1,), (0,)), ((), ()))
NT = (((1,), (1,)), ((), ()))
TN = (((0,), (0,)), ((), ()))


def dot(a, b, dims):
    return lax.dot_general(a, b, dims, preferred_element_type=f32)


def pack(x):
    high = x.astype(bf16)
    return jnp.concatenate([high, (x - high.astype(f32)).astype(bf16)], axis=1)


def halves(x):
    return x[:, :D] + x[:, D:]


def nn(a, b):
    return halves(dot(a, jnp.concatenate([b, b], axis=0), NN))


def nt(a, b):
    high, low = b[:, :D], b[:, D:]
    rows_high = jnp.concatenate([high, high], axis=1)
    rows_low = jnp.concatenate([low, low], axis=1)
    return halves(dot(a, jnp.concatenate([rows_high, rows_low], axis=0), NT))


def tn(a, b):
    stacked = jnp.concatenate([a[:, :D], a[:, D:]], axis=0)
    return halves(dot(stacked, jnp.concatenate([b, b], axis=0), TN))


def tn_long(a, b):
    x = dot(a, b, TN)
    return halves(x[:D] + x[D:])


def iota(axis):
    return lax.broadcasted_iota(jnp.int32, (BL, BL), axis)


def causal():
    return iota(0) >= iota(1)


def centred_sum_matrix():
    t, s = iota(0), iota(1)
    later = ((s <= t) & (s >= HALF)).astype(f32)
    earlier = ((s > t) & (s < HALF)).astype(f32)
    return (later - earlier).astype(bf16)


def rows(b):
    return slice(b * BL, (b + 1) * BL)


def value_tables(value_log):
    steps = (iota(0) - (HALF - 1)).astype(f32) * value_log
    return jnp.exp(steps), jnp.exp(-steps)


def cols(h, width=D):
    return slice(h * width, (h + 1) * width)


def last_row(b):
    return slice((b + 1) * BL - 1, (b + 1) * BL)


def before_and_after(c_ref, mid_ref, h, blocks):
    ends = [c_ref[last_row(b), cols(h)] for b in range(blocks)]
    mids = [mid_ref[h, b : b + 1] for b in range(blocks)]
    before, total = [], jnp.zeros((1, D), f32)
    for b in range(blocks):
        before.append(total + mids[b])
        total = before[b] + ends[b]
    after, rest = [None] * blocks, jnp.zeros((1, D), f32)
    for b in reversed(range(blocks)):
        after[b] = rest + ends[b]
        rest = after[b] + mids[b]
    steps = [jnp.exp(ends[b] + mids[b + 1]) for b in range(blocks - 1)]
    return before, after, steps


def columns_of(row_list):
    stacked = jnp.concatenate(row_list, axis=0)
    padded = jnp.concatenate([stacked, jnp.zeros((D - stacked.shape[0], D), f32)], axis=0)
    return jnp.transpose(padded)


def centred_sums(blocks, ld_ref, c_ref, h):
    matrix = centred_sum_matrix()
    matrix = jnp.concatenate([matrix, matrix], axis=1)
    mids = []
    for b in range(0, blocks, 2):
        x, y = pack(ld_ref[rows(b), cols(h)]), pack(ld_ref[rows(b + 1), cols(h)])
        right = jnp.concatenate(
            [
                jnp.concatenate([x[:, :D], y[:, :D]], axis=1),
                jnp.concatenate([x[:, D:], y[:, D:]], axis=1),
            ],
            axis=0,
        )
        c = dot(matrix, right, NN)
        for at in range(2):
            c_at = c[:, cols(at)]
            c_ref[rows(b + at), cols(h)] = c_at
            first = (b + at) * BL
            mids.append(ld_ref[first : first + 1, cols(h)] - c_at[0:1])
    return mids


def state_kernel(blocks, k_ref, v_ref, ld_ref, rate_ref, pay_ref, c_s, kk, vv):
    span = blocks * BL
    all_mids = [centred_sums(blocks, ld_ref, c_s, h) for h in range(TOGETHER)]
    for h in range(TOGETHER):
        value_log = -rate_ref[h]
        _, shrink = value_tables(value_log)
        rest = jnp.zeros((1, D), f32)
        for b in reversed(range(blocks)):
            c = c_s[rows(b), cols(h)]
            after = rest + c[BL - 1 : BL]
            rest = after + all_mids[h][b]
            kk[h, rows(b)] = pack(k_ref[rows(b), cols(h)].astype(f32) * jnp.exp(after - c))
            reach = jnp.exp(value_log * float(span - BL * b - HALF))
            vv[h, rows(b)] = pack(v_ref[rows(b), cols(h)].astype(f32) * (shrink * reach))
        total = tn_long(kk[h], vv[h])
        value_total = value_log * float(span)
        for part in range(4):
            pay_ref[4 * h + part, 0:32] = total[32 * part : 32 * part + 32]
            pay_ref[4 * h + part, 32:40] = jnp.concatenate(
                [pltpu.roll(rest, (D - 32 * part) % D, 1), value_total, jnp.zeros((6, D), f32)],
                axis=0,
            )


def local_kernel(
    blocks, made, q_ref, k_ref, v_ref, ld_ref, rate_ref, *rest
):
    core_ref, qd_ref, starts_ref, c_ref, mid_ref, qs, ks, vs, scores, kv = rest[made:]
    mask = causal()
    tables = []
    for h in range(TOGETHER):
        mids = centred_sums(blocks, ld_ref, c_ref, h)
        mid_ref[h] = jnp.concatenate(mids, axis=0)
    for h in range(TOGETHER):
        grow, shrink = value_tables(-rate_ref[h])
        before, _, steps = before_and_after(c_ref, mid_ref, h, blocks)
        tables.append((grow, steps))
        for b in range(blocks):
            c = c_ref[rows(b), cols(h)]
            q = q_ref[rows(b), cols(h)].astype(f32) * jnp.exp(c)
            qs[rows(b), cols(h, 2 * D)] = pack(q)
            qd_ref[rows(b), cols(h, 2 * D)] = pack(q * jnp.exp(before[b]))
            ks[rows(b), cols(h, 2 * D)] = pack(k_ref[rows(b), cols(h)].astype(f32) * jnp.exp(-c))
            vs[rows(b), cols(h, 2 * D)] = pack(v_ref[rows(b), cols(h)].astype(f32) * shrink)
    for h in range(TOGETHER):
        for b in range(blocks):
            part = nt(qs[rows(b), cols(h, 2 * D)], ks[rows(b), cols(h, 2 * D)])
            scores[rows(b), cols(h, 2 * D)] = pack(jnp.where(mask, part, 0.0))
    for h in range(TOGETHER):
        for b in range(blocks - 1):
            kv[h, b] = tn(ks[rows(b), cols(h, 2 * D)], vs[rows(b), cols(h, 2 * D)])
    for h in range(TOGETHER):
        key_steps = columns_of(tables[h][1])
        value_step = jnp.exp(-rate_ref[h] * float(BL))
        state = jnp.zeros((D, D), f32)
        for b in range(blocks):
            starts_ref[h, b] = state
            if b < blocks - 1:
                state = (state + kv[h, b]) * (key_steps[:, b : b + 1] * value_step)
    for h in range(TOGETHER):
        for b in range(blocks):
            value, state = vs[rows(b), cols(h, 2 * D)], pack(starts_ref[h, b])
            left = jnp.concatenate([scores[rows(b), cols(h, 2 * D)], qs[rows(b), cols(h, 2 * D)]], axis=1)
            right = jnp.concatenate([value, value, state, state], axis=0)
            core_ref[rows(b), cols(h)] = tables[h][0] * halves(dot(left, right, NN))


def core_kernel(
    blocks, turns, qd_ref, local_ref, grad_ref, state_ref, rate_ref, gain_ref,
    near_ref, near_qd_ref, near_grad_ref, sums_ref, squares, crosses,
):
    turn = pl.program_id(0)
    near_qd_ref[...] = qd_ref[...]
    near_grad_ref[...] = grad_ref[...]

    @pl.when(turn == 0)
    def _():
        squares[...] = jnp.zeros_like(squares)
        crosses[...] = jnp.zeros_like(crosses)

    grows, rights = [], []
    for h in range(TOGETHER):
        grows.append(value_tables(-rate_ref[h])[0])
        state = pack(state_ref[h])
        rights.append(jnp.concatenate([state, state], axis=0))
    for b in range(blocks):
        square, cross = squares[rows(b)], crosses[rows(b)]
        for h in range(TOGETHER):
            reach = jnp.exp(-rate_ref[h] * float(BL * b + HALF))
            incoming = halves(dot(qd_ref[rows(b), cols(h, 2 * D)], rights[h], NN))
            core = local_ref[rows(b), cols(h)] + (grows[h] * reach) * incoming
            near_ref[rows(b), cols(h)] = core
            square = square + core * core
            cross = cross + core * (grad_ref[rows(b), cols(h)].astype(f32) * gain_ref[h])
        squares[rows(b)] = square
        crosses[rows(b)] = cross

    @pl.when(turn == turns - 1)
    def _():
        ones = jnp.ones((8, 2 * D), bf16)
        for at, ref in enumerate((squares, crosses)):
            found = [dot(ones, pack(ref[rows(b)]), NT)[0:1] for b in range(blocks)]
            all_found = jnp.concatenate(found, axis=0)
            for copy in range(sums_ref.shape[0]):
                sums_ref[copy, at * blocks : (at + 1) * blocks] = all_found


def grad_kernel(
    blocks, qd_ref, core_ref, grad_ref, rate_ref, gain_ref, *rest
):
    *sums_refs, pay_ref, factor_ref, kept_ref, gg = rest
    turn = pl.program_id(0)
    columns = HEADS * D

    @pl.when(turn == 0)
    def _():
        both = sums_refs[0][0]
        for ref in sums_refs[1:]:
            both = both + ref[0]
        rms = lax.rsqrt(both[0:blocks] / columns + 1e-06)
        coef = rms * rms * rms * both[blocks : 2 * blocks] / columns
        for b in range(blocks):
            factor_ref[rows(b), :D] = jnp.transpose(jnp.broadcast_to(rms[b : b + 1], (BL, D)))
            factor_ref[rows(b), D:] = jnp.transpose(jnp.broadcast_to(coef[b : b + 1], (BL, D)))

    for h in range(TOGETHER):
        grow, _ = value_tables(-rate_ref[h])
        gain_sum = jnp.zeros((BL, D), f32)
        for b in range(blocks):
            core = core_ref[rows(b), cols(h)]
            kept_ref[rows(b), cols(h)] = core
            out = grad_ref[rows(b), cols(h)].astype(f32) * factor_ref[rows(b), :D]
            gain_sum = gain_sum + out * core
            g = out * gain_ref[h] - core * factor_ref[rows(b), D:]
            reach = jnp.exp(-rate_ref[h] * float(BL * b + HALF))
            gg[h, rows(b)] = pack(g * (grow * reach))
        total = tn_long(qd_ref[:, cols(h, 2 * D)], gg[h])
        gain_row = jnp.sum(gain_sum, axis=0, keepdims=True)
        for part in range(4):
            pay_ref[4 * h + part, 0:32] = total[32 * part : 32 * part + 32]
            pay_ref[4 * h + part, 32:40] = jnp.concatenate(
                [gain_row, jnp.zeros((7, D), f32)], axis=0
            )


def block_grad_kernel(
    blocks, made, qs, ks, vs, scores, c_ref, mid_ref, core_ref, grad_ref, factor_ref,
    starts_ref, state_ref, rate_ref, gain_ref, *rest,
):
    dq_ref, dk_ref, dv_ref, gs, start, mixed, qg, passed = rest[made:]
    mask = causal()
    tables = []
    for h in range(TOGETHER):
        grow, shrink = value_tables(-rate_ref[h])
        before, _, steps = before_and_after(c_ref, mid_ref, h, blocks)
        key_columns = columns_of(steps + [jnp.exp(x) for x in before])
        tables.append((shrink, key_columns))
        for b in range(blocks):
            out = grad_ref[rows(b), cols(h)].astype(f32) * factor_ref[rows(b), :D]
            g = out * gain_ref[h] - core_ref[rows(b), cols(h)] * factor_ref[rows(b), D:]
            gs[h, rows(b)] = pack(g * grow)
            at = blocks - 1 + b
            reach = jnp.exp(-rate_ref[h] * float(BL * b + HALF))
            begun = starts_ref[h, b] + state_ref[h] * (key_columns[:, at : at + 1] * reach)
            start[h, rows(b)] = pack(begun)
    for h in range(TOGETHER):
        for b in range(blocks):
            part = nt(gs[h, rows(b)], vs[rows(b), cols(h, 2 * D)])
            mixed[h, rows(b)] = pack(jnp.where(mask, part, 0.0))
    for h in range(TOGETHER):
        for b in range(1, blocks):
            qg[h, b] = tn(qs[rows(b), cols(h, 2 * D)], gs[h, rows(b)])
    for h in range(TOGETHER):
        value_step = jnp.exp(-rate_ref[h] * float(BL))
        now = jnp.zeros((D, D), f32)
        for b in reversed(range(blocks)):
            passed[h, rows(b)] = pack(now)
            if b:
                now = (now + qg[h, b]) * (tables[h][1][:, b - 1 : b] * value_step)
    for h in range(TOGETHER):
        for b in range(blocks):
            dq = nn(mixed[h, rows(b)], ks[rows(b), cols(h, 2 * D)]) + nt(gs[h, rows(b)], start[h, rows(b)])
            dq_ref[rows(b), cols(h)] = (jnp.exp(c_ref[rows(b), cols(h)]) * dq).astype(bf16)
    for h in range(TOGETHER):
        for b in range(blocks):
            dk = tn(mixed[h, rows(b)], qs[rows(b), cols(h, 2 * D)]) + nt(vs[rows(b), cols(h, 2 * D)], passed[h, rows(b)])
            dk_ref[rows(b), cols(h)] = jnp.exp(-c_ref[rows(b), cols(h)]) * dk
    for h in range(TOGETHER):
        for b in range(blocks):
            dv = tn(scores[rows(b), cols(h, 2 * D)], gs[h, rows(b)]) + nn(ks[rows(b), cols(h, 2 * D)], passed[h, rows(b)])
            dv_ref[rows(b), cols(h)] = tables[h][0] * dv


def final_kernel(
    blocks, k_ref, v_ref, c_ref, mid_ref, dk_ref, dv_ref, back_ref, rate_ref,
    dk_out, dv_out, gain_out,
):
    span = blocks * BL
    for h in range(TOGETHER):
        value_log = -rate_ref[h]
        _, shrink = value_tables(value_log)
        _, after, _ = before_and_after(c_ref, mid_ref, h, blocks)
        back = pack(back_ref[4 * h : 4 * h + 4, 0:32].reshape(D, D))
        for b in range(blocks):
            at = rows(b), cols(h)
            fade = jnp.exp(after[b] - c_ref[at])
            value_fade = shrink * jnp.exp(value_log * float(span - BL * b - HALF))
            ks = pack(k_ref[at].astype(f32) * fade)
            vs = pack(v_ref[at].astype(f32) * value_fade)
            dk_out[at] = (dk_ref[at] + fade * nt(vs, back)).astype(bf16)
            dv_out[at] = (dv_ref[at] + value_fade * nn(ks, back)).astype(bf16)
        gain_out[h] = back_ref[4 * h, 32:33]


def key_weights(count, extra_ref):
    decays = jnp.concatenate([extra_ref[s, 0:1] for s in range(count)], axis=0)
    padded = jnp.concatenate([decays, jnp.zeros((D - count, D), f32)], axis=0)
    return jnp.exp(jnp.transpose(padded)[0:32]), jnp.exp(extra_ref[0, 1:2])


def forward_scan_kernel(count, pay_ref, extra_ref, out_ref):
    key_columns, value_row = key_weights(count, extra_ref)
    state = jnp.zeros((32, D), f32)
    for s in range(count):
        out_ref[s] = state
        state = (key_columns[:, s : s + 1] * value_row) * state + pay_ref[s]


def backward_scan_kernel(count, scale, pay_ref, gain_ref, extra_ref, out_ref):
    key_columns, value_row = key_weights(count, extra_ref)
    state = jnp.zeros((32, D), f32)
    gain = jnp.zeros((EXTRA, D), f32)
    for s in range(count):
        gain = gain + gain_ref[s]
    gain = gain * scale
    for s in reversed(range(count)):
        out_ref[s, 0:32] = state
        out_ref[s, 32:40] = gain
        state = (key_columns[:, s : s + 1] * value_row) * state + pay_ref[s]


def on_device(queries, keys, values, out_grad, log_key_decay, value_rate, norm_gain):
    tokens, width = queries.shape
    heads = width // D
    blocks = tokens // BL
    around = ("outer", "inner")
    count = lax.axis_size("outer") * lax.axis_size("inner")
    head_count = lax.axis_size("head")
    rate = value_rate.reshape(heads, 1, D)
    gain = norm_gain.reshape(heads, 1, D)
    chunks = heads * 4

    turns = heads // TOGETHER

    def specs(first):
        wide = pl.BlockSpec((tokens, TOGETHER * D), lambda h: (0, h + first))
        pair = pl.BlockSpec((tokens, TOGETHER * 2 * D), lambda h: (0, h + first))
        row = pl.BlockSpec((TOGETHER, 1, D), lambda h: (h + first, 0, 0))
        eight = pl.BlockSpec((TOGETHER, blocks, D), lambda h: (h + first, 0, 0))
        square = pl.BlockSpec((TOGETHER, D, D), lambda h: (h + first, 0, 0))
        many = pl.BlockSpec((TOGETHER, blocks, D, D), lambda h: (h + first, 0, 0, 0))
        payload = pl.BlockSpec((TOGETHER * 4, 32 + EXTRA, D), lambda h: (h + first, 0, 0))
        return wide, pair, row, eight, square, many, payload

    wide, pair, row, eight, square, many, payload = specs(0)
    factors = pl.BlockSpec((tokens, 2 * D), lambda h: (0, 0))
    packed = pltpu.VMEM((TOGETHER, tokens, 2 * D), bf16)
    squares = pltpu.VMEM((TOGETHER, blocks, D, D), f32)
    sums_spec = pl.BlockSpec((1, 2 * blocks, D), lambda h: (0, 0, 0))

    def shape(*dims, dtype=f32):
        return jax.ShapeDtypeStruct(dims, dtype)

    wide_shape = shape(tokens, width)
    wide_low = shape(tokens, width, dtype=bf16)
    pair_shape = shape(tokens, 2 * width, dtype=bf16)
    pay_shape = shape(chunks, 32 + EXTRA, D)
    def hbm(*arrays):
        return [pltpu.with_memory_space_constraint(x, pltpu.HBM) for x in arrays]

    def call(body, name, ins, outs, out_shape, scratch=(), flops=0, steps=turns, aliases={}, limit=VMEM_MIB):
        return pl.pallas_call(
            body, name=name, grid=(steps,), in_specs=ins, out_specs=outs, out_shape=out_shape,
            scratch_shapes=list(scratch), input_output_aliases=aliases,
            compiler_params=pltpu.CompilerParams(
                dimension_semantics=("arbitrary",), vmem_limit_bytes=limit * 1024 * 1024
            ),
            cost_estimate=pl.CostEstimate(
                flops=flops, transcendentals=0, bytes_accessed=16 * 1024 * 1024
            ),
        )

    pay = call(
        functools.partial(state_kernel, blocks), "state", [wide, wide, wide, row],
        payload, pay_shape,
        [pltpu.VMEM((tokens, TOGETHER * D), f32), packed, packed],
    )(keys, values, log_key_decay, rate)
    got = lax.all_to_all(pay, around, 0, 0)
    half = turns // 2
    made = ()
    for part in range(2):
        w, p, r, e, s, m, _ = specs(part * half)
        made = call(
            functools.partial(local_kernel, blocks, len(made)), f"local{part}",
            [w, w, w, w, r] + [pl.BlockSpec(memory_space=pl.ANY)] * len(made),
            [w, p, m, w, e, p, p, p, p],
            [
                wide_shape, pair_shape, shape(heads, blocks, D, D), wide_shape,
                shape(heads, blocks, D), pair_shape, pair_shape, pair_shape, pair_shape,
            ],
            [squares], flops=10**10, steps=half, aliases={5 + i: i for i in range(len(made))},
        )(queries, keys, values, log_key_decay, rate, *made)
    local, qd, starts, c, mid, qs, ks, vs, scores = made
    top = pl.BlockSpec((count, 32, D), lambda i: (0, 0, 0))
    bottom = pl.BlockSpec((count, EXTRA, D), lambda i: (0, 32 // EXTRA, 0))
    full = pl.BlockSpec((count, 32 + EXTRA, D), lambda i: (0, 0, 0))
    small = pltpu.CompilerParams(
        dimension_semantics=("arbitrary",), vmem_limit_bytes=8 * 1024 * 1024
    )
    prefixes = pl.pallas_call(
        functools.partial(forward_scan_kernel, count), name="fscan", grid=(1,),
        in_specs=[top, bottom], out_specs=top, out_shape=shape(chunks, 32, D),
        compiler_params=small,
    )(got, got)
    state_in = lax.all_to_all(prefixes, around, 0, 0).reshape(heads, D, D)
    near, near_qd, near_grad, sums = call(
        functools.partial(core_kernel, blocks, turns), "core",
        [pair, wide, wide, square, row, row], [wide, pair, wide, sums_spec],
        [
            wide_shape, pair_shape, wide_low, shape(1, 2 * blocks, D),
        ],
        [pltpu.VMEM((tokens, D), f32)] * 2, limit=24,
    )(*hbm(qd, local, out_grad), state_in, rate, gain)
    all_sums = [sums] + [
        lax.ppermute(sums, "head", [(i, i ^ step) for i in range(head_count)])
        for step in (1, 3, 2)
    ]
    back_pay, factor, core = call(
        functools.partial(grad_kernel, blocks), "grad",
        [pair, wide, wide, row, row] + [sums_spec] * head_count, [payload, factors, wide],
        [pay_shape, pltpu.HBM((tokens, 2 * D), f32), pltpu.HBM(wide_shape.shape, f32)],
        [packed], limit=24,
    )(near_qd, near, near_grad, rate, gain, *all_sums)
    back_got = lax.all_to_all(back_pay, around, 0, 0)
    made = ()
    for part in range(2):
        w, p, r, e, s, m, _ = specs(part * half)
        made = call(
            functools.partial(block_grad_kernel, blocks, len(made)), f"blockgrad{part}",
            [p, p, p, p, w, e, w, w, factors, m, s, r, r]
            + [pl.BlockSpec(memory_space=pl.ANY)] * len(made),
            [w, w, w], [wide_low, wide_shape, wide_shape],
            [packed] * 3 + [squares, packed], flops=10**10, steps=half,
            aliases={13 + i: i for i in range(len(made))},
        )(
            qs, ks, vs, scores, c, mid, core, out_grad, factor, starts, state_in, rate, gain,
            *made,
        )
    dq, dk_local, dv_local = made
    scale = 1.0 / math.sqrt(tokens * count)
    back_prefixes = pl.pallas_call(
        functools.partial(backward_scan_kernel, count, scale), name="bscan", grid=(1,),
        in_specs=[top, bottom, bottom], out_specs=full, out_shape=pay_shape,
        compiler_params=small,
    )(back_got, back_got, got)
    back_in = lax.all_to_all(back_prefixes, around, 0, 0)
    dk, dv, gain_grad = call(
        functools.partial(final_kernel, blocks), "final",
        [wide, wide, wide, eight, wide, wide, payload, row], [wide, wide, row],
        [wide_low, wide_low, shape(heads, 1, D)], limit=24,
    )(*hbm(keys, values, c), mid, *hbm(dk_local, dv_local), back_in, rate)
    return dq, dk, dv, gain_grad.reshape(width)


def solution(mesh):
    spec = P(("outer", "inner"), "head")
    return jax.shard_map(
        on_device,
        mesh=mesh,
        in_specs=(spec, spec, spec, spec, spec, P("head"), P("head")),
        out_specs=(spec, spec, spec, P("head")),
        check_vma=False,
    )
```
